32 devices in a mesh: panel: 2 (over y), row: 4 (over z), layer: 4 (over x, core).
Axes of the slice: x: 2, y: 2, z: 4, core: 2. Of those that a mesh axis runs over, the one named last changes fastest.
Arguments:
- layers: bfloat16 [4, 8192, 512], P('layer', 'row', 'panel'), parts along dimension 2, may hold values from -6 to 6
- table: bfloat16 [16, 128, 64], replicated, may hold values from -0.375 to 0.375
- fitting: bfloat16 [8192, 6600], P('row', 'layer'), may hold values from -0.09375 to 0.09375
- owner: int32 [4, 128, 1], P('layer', 'row'), may hold values from 0 to 3; in each aligned block of 32 rows (0 to 31, 32 to 63, ..., all dimensions but the last counted through in order) at most 16 rows name the same one
- local_slice: int32 [4, 128], P('layer', 'row'), may hold values from 0 to 15
- block_index: int32 [4, 128], P('layer', 'row'), may hold values from 0 to 31
- weight_index: int32 [4, 128], P('layer', 'row'), may hold values from 0 to 15
Outputs:
- actuators: bfloat16 [512, 6600], P(('panel', 'row'), 'layer'), parts along dimension 0
The draws below stay inside these ranges and needn't reach their ends.
There are 2 independent parts, one for each index of `panel`. The reference program is written for one: setup_inputs(seed, part) draws one part's arguments, and reference() takes and returns one part's arrays. A program takes and returns all parts, laid end to end along the dimension named above; an argument that names none is the same for every part. Nothing has to cross between parts.
Inputs may be any that keep to these rules, and one draw needn't show every extreme that they name: `owner`: within the 32 entries of one layer on one row device (aligned blocks of 32 entries), no value is named more than 16 times, and in every draw some block names one value exactly 16 times.
All inputs are finite; a program needn't handle non-finite values.
Results may differ from the reference program's by a relative error of at most 0.0058.
Values may be sent and summed in bfloat16 or wider, within the bound.
A program may use at most 64 MiB of HBM per device.

```python
import math
import jax
import jax.numpy as jnp
import numpy as np
from jax import lax

C = 256
NA = 6600
S = 128
B = 64
K = 16
SL_DEV = 16
E_DEV = 32
NL = 4
NP = 8192
NB = 32
NS = 64
NQ = 8192
ENT = 128
CAP = 16
N_ROW = 4


def touch_ends(result, rng, smallest, largest):
    place = [jax.random.randint(jax.random.fold_in(rng, axis), (), 0, length) for axis, length in enumerate(result.shape)]
    longest = result.shape.index(max(result.shape))
    beside = place[:longest] + [(place[longest] + 1) % result.shape[longest]] + place[longest + 1:]
    return result.at[tuple(place)].set(smallest).at[tuple(beside)].set(largest)


def raised(values, stream_key, source, target, parts, factor):
    def block_of(dim):
        return (jnp.arange(values.shape[dim]) // (values.shape[dim] // parts)).reshape((-1,) + (1,) * (values.ndim - 1 - dim))

    one_side = jax.random.permutation(stream_key, parts)[block_of(target)]
    other_side = (block_of(target) + parts // 2) % parts
    return jnp.where((block_of(source) == one_side) | (block_of(source) == other_side), factor * values, values)


def steps_of(key, shape, cuts, low, largest):
    loudness, own = 1.0, jax.random.fold_in(key, 6)
    for axis_at, shards_of in cuts:
        heights = jnp.exp(jax.random.uniform(jax.random.fold_in(own, axis_at), (shards_of,), jnp.float32, low / len(cuts), largest / len(cuts)))
        loudness = loudness * jnp.repeat(heights, shape[axis_at] // shards_of).reshape([-1 if axis == axis_at else 1 for axis in range(len(shape))])
    return loudness


def routed_block(key, own, number, rows, count, top, reach, slope):
    sequence = jax.random.permutation(key, count)
    crowded, common = load_shares(count, rows * top, reach, slope, True), load_shares(count, rows * top, reach, slope, False)
    places = jnp.arange(count)

    def named(sizes, turn):
        used = int((sizes > 0).sum())
        fixed = max(1, used // 4)
        passed = fixed + (places - fixed + turn * (used - fixed)) % max(1, count - fixed)
        return jnp.zeros((count,), jnp.int32).at[sequence[jnp.where(places < fixed, places, passed)]].set(jnp.asarray(sizes, jnp.int32))

    sizes = jnp.where(number % 4 == 0, named(crowded, number // 4), named(common, number - number // 4 - 1))
    mixed = jax.random.permutation(jax.random.fold_in(own, 3), count)
    source_of, receiver = mixed[0:count // 2 * 2:2], mixed[1:count // 2 * 2:2]
    slack = jnp.minimum(sizes[source_of] - 1, reach - sizes[receiver]) // 2
    slack = jnp.where((source_of == sequence[0]) | (receiver == sequence[0]) | (sizes[receiver] == 0), 0, jnp.maximum(slack, 0))
    passed = jax.random.randint(jax.random.fold_in(own, 4), (count // 2,), 0, 1 << 20) % (slack + 1)
    sizes = sizes.at[source_of].add(-passed).at[receiver].add(passed)
    labels = jnp.searchsorted(jnp.cumsum(sizes), jnp.arange(rows * top), side="right").astype(jnp.int32)
    grid = labels.reshape(top, rows).T
    grid = grid[jax.random.permutation(jax.random.fold_in(own, 1), rows)]
    turn = jax.random.randint(jax.random.fold_in(own, 2), (rows, 1), 0, top)
    return jnp.take_along_axis(grid, (jnp.arange(top)[None, :] + turn) % top, axis=1)


def load_shares(amount, total, most, slope, full):
    loads = [(1 << 20) // math.isqrt(grade ** slope) + 1 for grade in range(1, amount + 1)]
    largest = most if full else min(most, max(-(-total // amount), total * loads[0] // sum(loads)))
    least = 1 if total - largest >= amount - 1 else 0
    holding, rest = [largest] + [least] * (amount - 1), total - largest - least * (amount - 1)
    while rest > 0:
        movable = [i for i in range(1, amount) if holding[i] < largest] or [i for i in range(1, amount) if holding[i] < most]
        pool, left = sum([loads[i] for i in movable]), rest
        for i in movable:
            extra = min(most - holding[i], max(1, left * loads[i] // pool), rest)
            holding[i] = holding[i] + extra
            rest = rest - extra
    return np.array(holding)


def centred(stream_key, shape, deviation, most, pieces=(), kind=jnp.bfloat16):
    loudness = steps_of(stream_key, shape, pieces, -0.22, 0.18) if pieces else 1.0
    drawn = jax.random.normal(stream_key, shape, jnp.float32) * deviation * loudness
    return jnp.minimum(jnp.maximum(drawn, -most), most).astype(kind)


def gaussian_with(key, dims, width, limit, pieces, heavy, held_as=jnp.bfloat16):
    values = width * jax.random.normal(key, dims, jnp.float32)
    if pieces:
        values = values * steps_of(key, dims, pieces, -0.22, 0.18)
    return jnp.clip(raised(values, jax.random.fold_in(key, 3), *heavy), -limit, limit).astype(held_as)


def setup_inputs(seed: int = 0, part: int = 0) -> dict:
    splits = jax.random.split(jax.random.key(seed), 8)
    part_keys = jax.random.split(jax.random.fold_in(splits[7], part), 8)
    layers = centred(part_keys[0], (NL, NP, C), 1.0, 6.0, ((0, 4), (1, 4)))
    table = centred(splits[1], (K, S, B), (4 * B) ** -0.5, 0.375)
    fitting = gaussian_with(splits[2], (NQ, NA), NQ ** -0.5, 0.09375, ((0, 4), (1, 4)), (0, 1, 4, 2.0))
    owner_keys = jax.random.split(jax.random.fold_in(splits[3], 1), NL * ENT // E_DEV)
    owner_turns = jax.random.permutation(jax.random.fold_in(splits[3], 3), NL * ENT // E_DEV)
    owner = jax.vmap(lambda own, number: routed_block(jax.random.fold_in(splits[3], 2), own, number, E_DEV, N_ROW, 1, CAP, 2))(owner_keys, owner_turns).reshape((NL, ENT, 1))
    local_slice = touch_ends(jax.random.randint(splits[4], (NL, ENT), 0, SL_DEV), jax.random.fold_in(splits[4], 1), 0, SL_DEV - 1).astype(jnp.int32)
    block_index = touch_ends(jax.random.randint(splits[5], (NL, ENT), 0, NB), jax.random.fold_in(splits[5], 1), 0, NB - 1).astype(jnp.int32)
    weight_index = touch_ends(jax.random.randint(splits[6], (NL, ENT), 0, K), jax.random.fold_in(splits[6], 1), 0, K - 1).astype(jnp.int32)
    return {"layers": layers, "table": table, "fitting": fitting, "owner": owner, "local_slice": local_slice, "block_index": block_index, "weight_index": weight_index}


def reference(layers, table, fitting, owner, local_slice, block_index, weight_index):
    layer_total = layers.shape[0]

    def one_layer(running, layer_index):
        layer_rows = lax.dynamic_index_in_dim(layers, layer_index, 0, keepdims=False)
        owner_now = lax.dynamic_index_in_dim(owner, layer_index, 0, keepdims=False)[:, 0]
        local_now = lax.dynamic_index_in_dim(local_slice, layer_index, 0, keepdims=False)
        block_now = lax.dynamic_index_in_dim(block_index, layer_index, 0, keepdims=False)
        weight_now = lax.dynamic_index_in_dim(weight_index, layer_index, 0, keepdims=False)
        source_dev = (jnp.arange(ENT, dtype=jnp.int32) // E_DEV).astype(jnp.int32)
        start_block = (source_dev * NB + block_now).astype(jnp.int32)
        grouped = layer_rows.reshape(NB * N_ROW, B, C)
        picked = grouped[start_block].astype(jnp.float32)
        weights = table[weight_now].astype(jnp.float32)
        term = jnp.einsum("esb,ebc->esc", weights, picked).astype(jnp.bfloat16)
        destination = (owner_now * SL_DEV + local_now).astype(jnp.int32)
        running = running + jax.ops.segment_sum(term.astype(jnp.float32), destination, num_segments=NS)
        return running, None

    pupil, _ = lax.scan(one_layer, jnp.zeros((NS, S, C), jnp.float32), jnp.arange(layer_total, dtype=jnp.int32))
    pupil_rounded = pupil.reshape(NQ, C).astype(jnp.bfloat16)
    return jnp.dot(pupil_rounded.T, fitting, preferred_element_type=jnp.float32).astype(jnp.bfloat16)
```

```python
import jax
import jax.numpy as jnp
from jax import lax
from jax.experimental import pallas as pl
from jax.experimental.pallas import tpu as pltpu
from jax.sharding import PartitionSpec as P


def local_rows(layers, table, fitting, owner, local_slice, block_index, weight_index):
    rows_dev = layers.shape[1]
    columns = layers.shape[2]
    slice_rows = table.shape[1]
    block_rows = table.shape[2]
    entries = owner.shape[1]
    peer_count = lax.axis_size("row")
    capacity = max(2, 2 * entries // peer_count)
    slot_count = peer_count * capacity
    owned_slices = fitting.shape[0] // slice_rows
    owner_now = owner[0, :, 0]
    local_now = local_slice[0]
    owner_match = (owner_now[:, None] == jnp.arange(peer_count, dtype=jnp.int32)[None, :]).astype(
        jnp.int32
    )
    slot_rank = jnp.sum((jnp.cumsum(owner_match, axis=0) - 1) * owner_match, axis=1)
    target = owner_now * capacity + slot_rank
    placed = target[None, :] == jnp.arange(slot_count, dtype=jnp.int32)[:, None]
    filled = jnp.any(placed, axis=1)
    source = jnp.sum(jnp.where(placed, jnp.arange(entries, dtype=jnp.int32)[None, :], 0), axis=1)
    send_local = jnp.where(filled, local_now[source], -1).reshape(peer_count, capacity)
    grouped = layers[0].reshape(rows_dev // block_rows, block_rows, columns)
    picked = grouped[block_index[0][source]].reshape(peer_count, capacity, block_rows, columns)
    send_weight = weight_index[0][source].reshape(peer_count, capacity)
    got_rows, got_weight, got_local = (
        lax.all_to_all(picked, "row", split_axis=0, concat_axis=0, tiled=True),
        lax.all_to_all(send_weight, "row", split_axis=0, concat_axis=0, tiled=True),
        lax.all_to_all(send_local, "row", split_axis=0, concat_axis=0, tiled=True),
    )
    pupil_terms = jnp.einsum(
        "ksb,kbc->ksc",
        table[got_weight.reshape(-1)],
        got_rows.reshape(slot_count, block_rows, columns),
        preferred_element_type=jnp.float32,
    ).astype(jnp.bfloat16)
    selector = (
        jnp.arange(owned_slices, dtype=jnp.int32)[:, None] == got_local.reshape(-1)[None, :]
    ).astype(jnp.bfloat16)
    partial_pupil = jnp.dot(
        selector,
        pupil_terms.reshape(slot_count, slice_rows * columns),
        preferred_element_type=jnp.float32,
    ).reshape(owned_slices * slice_rows, columns)
    pupil_rounded = lax.psum(partial_pupil, "layer").astype(jnp.bfloat16)
    return lax.psum_scatter(
        lax.dot_general(
            pupil_rounded, fitting, (((0,), (0,)), ((), ())), preferred_element_type=jnp.float32
        ),
        "row",
        scatter_dimension=0,
        tiled=True,
    ).astype(jnp.bfloat16)


def terms_kernel(own_ref, got_ref, table_ref, meta_ref, out_ref, total_ref):
    entries = meta_ref.shape[2]
    block_rows = table_ref.shape[2]
    total_ref[...] = jnp.zeros_like(total_ref)
    group = 8 if entries % 8 == 0 else 1
    for part, rows_ref in enumerate((own_ref, got_ref)):

        def step(index, carry):
            terms = []
            for offset in range(group):
                entry = index * group + offset
                start = pl.multiple_of(meta_ref[part, 1, entry] * block_rows, block_rows)
                terms.append(
                    jnp.dot(
                        table_ref[meta_ref[part, 2, entry]],
                        rows_ref[pl.ds(start, block_rows), :],
                        preferred_element_type=jnp.float32,
                    )
                )
            for offset in range(group):
                place = meta_ref[part, 0, index * group + offset]
                total_ref[place] += terms[offset]
            return carry

        lax.fori_loop(0, entries // group, step, 0)

    def write(index, carry):
        out_ref[index] = total_ref[index].astype(out_ref.dtype)
        return carry

    lax.fori_loop(0, out_ref.shape[0], write, 0)


def local_reduced(layers, table, fitting, owner, local_slice, block_index, weight_index):
    columns = layers.shape[2]
    slice_rows = table.shape[1]
    peer_count = lax.axis_size("row")
    owned_slices = fitting.shape[0] // slice_rows
    half_slices = owned_slices // 2
    half_columns = columns // 2
    slice_total = peer_count * owned_slices
    me = lax.axis_index("layer")
    core = me % 2
    along = me // 2
    swap_x = [(0, 2), (2, 0), (1, 3), (3, 1)]
    swap_core = [(0, 1), (1, 0), (2, 3), (3, 2)]

    local_now = local_slice[0]
    place = (
        (local_now // half_slices) * (peer_count * half_slices)
        + owner[0, :, 0] * half_slices
        + local_now % half_slices
    )
    meta = jnp.stack([place, block_index[0], weight_index[0]])
    own = lax.dynamic_slice_in_dim(layers[0], along * half_columns, half_columns, 1)
    other = lax.dynamic_slice_in_dim(layers[0], (1 - along) * half_columns, half_columns, 1)
    got = lax.ppermute(other, "layer", swap_x)
    got_meta = lax.ppermute(meta, "layer", swap_x)
    partial = pl.pallas_call(
        terms_kernel,
        out_shape=jax.ShapeDtypeStruct((slice_total, slice_rows, half_columns), jnp.bfloat16),
        in_specs=[pl.BlockSpec(memory_space=pltpu.VMEM)] * 3
        + [pl.BlockSpec(memory_space=pltpu.SMEM)],
        out_specs=pl.BlockSpec(memory_space=pltpu.VMEM),
        scratch_shapes=[pltpu.VMEM((slice_total, slice_rows, half_columns), jnp.float32)],
    )(own, got, table, jnp.stack([meta, got_meta]))
    partial = partial.reshape(2, peer_count, half_slices * slice_rows, half_columns)
    kept = lax.dynamic_index_in_dim(partial, core, 0, keepdims=False)
    given = lax.dynamic_index_in_dim(partial, 1 - core, 0, keepdims=False)
    both = (
        kept.astype(jnp.float32) + lax.ppermute(given, "layer", swap_core).astype(jnp.float32)
    ).astype(jnp.bfloat16)
    arrived = lax.all_to_all(both, "row", split_axis=0, concat_axis=0, tiled=True)
    piece = jnp.sum(arrived.astype(jnp.float32), axis=0).astype(jnp.bfloat16)
    pieces = lax.all_gather(piece, "layer", axis=0, tiled=False)
    pupil_rounded = (
        pieces.reshape(2, 2, half_slices * slice_rows, half_columns)
        .transpose(1, 2, 0, 3)
        .reshape(owned_slices * slice_rows, columns)
    )
    product = lax.dot_general(
        pupil_rounded, fitting, (((0,), (0,)), ((), ())), preferred_element_type=jnp.float32
    ).astype(jnp.bfloat16)
    product = product.reshape(peer_count, columns // peer_count, fitting.shape[1])
    landed = lax.all_to_all(product, "row", split_axis=0, concat_axis=0, tiled=True)
    return jnp.sum(landed.astype(jnp.float32), axis=0).astype(jnp.bfloat16)


def local(layers, table, fitting, owner, local_slice, block_index, weight_index):
    arguments = (layers, table, fitting, owner, local_slice, block_index, weight_index)
    entries, peers, group = owner.shape[1], lax.axis_size("row"), lax.axis_size("layer")
    raw_rows = max(2, 2 * entries // peers) * table.shape[2]
    reduced_rows = fitting.shape[0] // group
    if group == 4 and raw_rows > reduced_rows:
        return local_reduced(*arguments)
    return local_rows(*arguments)


def solution(mesh):
    return jax.shard_map(
        local,
        mesh=mesh,
        in_specs=(
            P("layer", "row", "panel"),
            P(),
            P("row", "layer"),
            P("layer", "row", None),
            P("layer", "row"),
            P("layer", "row"),
            P("layer", "row"),
        ),
        out_specs=P(("panel", "row"), "layer"),
        check_vma=False,
    )
```

```python
import functools

import jax
import jax.numpy as jnp
from jax import lax
from jax.experimental import pallas as pl
from jax.experimental.pallas import tpu as pltpu

MESH = pl.DeviceIdType.MESH
from jax.sharding import PartitionSpec as P


def local_rows(layers, table, fitting, owner, local_slice, block_index, weight_index):
    rows_dev = layers.shape[1]
    columns = layers.shape[2]
    slice_rows = table.shape[1]
    block_rows = table.shape[2]
    entries = owner.shape[1]
    peer_count = lax.axis_size("row")
    capacity = max(2, 2 * entries // peer_count)
    slot_count = peer_count * capacity
    owned_slices = fitting.shape[0] // slice_rows
    owner_now = owner[0, :, 0]
    local_now = local_slice[0]
    owner_match = (owner_now[:, None] == jnp.arange(peer_count, dtype=jnp.int32)[None, :]).astype(
        jnp.int32
    )
    slot_rank = jnp.sum((jnp.cumsum(owner_match, axis=0) - 1) * owner_match, axis=1)
    target = owner_now * capacity + slot_rank
    placed = target[None, :] == jnp.arange(slot_count, dtype=jnp.int32)[:, None]
    filled = jnp.any(placed, axis=1)
    source = jnp.sum(jnp.where(placed, jnp.arange(entries, dtype=jnp.int32)[None, :], 0), axis=1)
    send_local = jnp.where(filled, local_now[source], -1).reshape(peer_count, capacity)
    grouped = layers[0].reshape(rows_dev // block_rows, block_rows, columns)
    picked = grouped[block_index[0][source]].reshape(peer_count, capacity, block_rows, columns)
    send_weight = weight_index[0][source].reshape(peer_count, capacity)
    got_rows, got_weight, got_local = (
        lax.all_to_all(picked, "row", split_axis=0, concat_axis=0, tiled=True),
        lax.all_to_all(send_weight, "row", split_axis=0, concat_axis=0, tiled=True),
        lax.all_to_all(send_local, "row", split_axis=0, concat_axis=0, tiled=True),
    )
    pupil_terms = jnp.einsum(
        "ksb,kbc->ksc",
        table[got_weight.reshape(-1)],
        got_rows.reshape(slot_count, block_rows, columns),
        preferred_element_type=jnp.float32,
    ).astype(jnp.bfloat16)
    selector = (
        jnp.arange(owned_slices, dtype=jnp.int32)[:, None] == got_local.reshape(-1)[None, :]
    ).astype(jnp.bfloat16)
    partial_pupil = jnp.dot(
        selector,
        pupil_terms.reshape(slot_count, slice_rows * columns),
        preferred_element_type=jnp.float32,
    ).reshape(owned_slices * slice_rows, columns)
    pupil_rounded = lax.psum(partial_pupil, "layer").astype(jnp.bfloat16)
    return lax.psum_scatter(
        lax.dot_general(
            pupil_rounded, fitting, (((0,), (0,)), ((), ())), preferred_element_type=jnp.float32
        ),
        "row",
        scatter_dimension=0,
        tiled=True,
    ).astype(jnp.bfloat16)


def terms_kernel(own_ref, got_ref, table_ref, meta_ref, out_ref, total_ref):
    entries = meta_ref.shape[2]
    block_rows = table_ref.shape[2]
    total_ref[...] = jnp.zeros_like(total_ref)
    group = 8 if entries % 8 == 0 else 1
    for part, rows_ref in enumerate((own_ref, got_ref)):

        def step(index, carry):
            terms = []
            for offset in range(group):
                entry = index * group + offset
                start = pl.multiple_of(meta_ref[part, 1, entry] * block_rows, block_rows)
                terms.append(
                    jnp.dot(
                        table_ref[meta_ref[part, 2, entry]],
                        rows_ref[pl.ds(start, block_rows), :],
                        preferred_element_type=jnp.float32,
                    )
                )
            for offset in range(group):
                place = meta_ref[part, 0, index * group + offset]
                total_ref[place] += terms[offset]
            return carry

        lax.fori_loop(0, entries // group, step, 0)

    def write(index, carry):
        out_ref[index] = total_ref[index].astype(out_ref.dtype)
        return carry

    lax.fori_loop(0, out_ref.shape[0], write, 0)


def exchange_kernel(
    peers, part_ref, fitting_ref, out_ref,
    fit, core_in, both, row_in, pieces, total, product, landed,
    fit_sem, core_send, core_recv, row_send, row_recv, layer_send, layer_recv, end_send, end_recv,
):
    row = lax.axis_index("row")
    me = lax.axis_index("layer")
    core = lax.rem(me, 2)
    steps = core_send.shape[0]
    piece_rows = pieces.shape[1]
    rows = piece_rows // steps
    width = fit.shape[1]
    half_columns = pieces.shape[2]
    out_rows = out_ref.shape[0]
    row_peers = [lax.rem(row + k, peers) for k in range(1, peers)]
    layer_peers = [lax.rem(me + k, 4) for k in range(1, 4)]

    fit_copy = pltpu.make_async_copy(fitting_ref, fit, fit_sem)
    fit_copy.start()
    barrier = pltpu.get_barrier_semaphore()
    for peer in row_peers:
        pl.semaphore_signal(barrier, inc=1, device_id={"row": peer}, device_id_type=MESH)
    for peer in layer_peers:
        pl.semaphore_signal(barrier, inc=1, device_id={"layer": peer}, device_id_type=MESH)
    pl.semaphore_wait(barrier, peers - 1 + 3)

    core_copies = []
    for step in range(steps):
        copy = pltpu.make_async_remote_copy(
            src_ref=part_ref.at[1 - core, :, pl.ds(step * rows, rows), :],
            dst_ref=core_in.at[:, pl.ds(step * rows, rows), :],
            send_sem=core_send.at[step],
            recv_sem=core_recv.at[step],
            device_id={"layer": me + 1 - 2 * core},
            device_id_type=MESH,
        )
        copy.start()
        core_copies.append(copy)

    row_copies = []
    for step in range(steps):
        part = slice(step * rows, (step + 1) * rows)
        core_copies[step].wait_recv()
        both[:, part, :] = (
            part_ref[core, :, part, :].astype(jnp.float32) + core_in[:, part, :].astype(jnp.float32)
        ).astype(both.dtype)
        sent = []
        for k, peer in enumerate(row_peers):
            copy = pltpu.make_async_remote_copy(
                src_ref=both.at[peer, pl.ds(step * rows, rows), :],
                dst_ref=row_in.at[k, pl.ds(step * rows, rows), :],
                send_sem=row_send.at[k, step],
                recv_sem=row_recv.at[k, step],
                device_id={"row": peer},
                device_id_type=MESH,
            )
            copy.start()
            sent.append(copy)
        row_copies.append(sent)

    tiles = [(start, min(start + 512, width)) for start in range(0, width, 512)]

    def multiply(step):
        for start, stop in tiles:
            value = None
            for half in range(2):
                part = slice(step * rows, (step + 1) * rows)
                left = jnp.concatenate([pieces[half, part, :], pieces[2 + half, part, :]], axis=1)
                first = half * piece_rows + step * rows
                term = lax.dot_general(
                    left,
                    fit[first : first + rows, start:stop],
                    (((0,), (0,)), ((), ())),
                    preferred_element_type=jnp.float32,
                )
                value = term if value is None else value + term
            if step == 0:
                total[:, start:stop] = value
            else:
                total[:, start:stop] += value

    layer_copies = []
    for step in range(steps):
        part = slice(step * rows, (step + 1) * rows)
        for copy in row_copies[step]:
            copy.wait_recv()
        value = both[row, part, :].astype(jnp.float32)
        for k in range(peers - 1):
            value = value + row_in[k, part, :].astype(jnp.float32)
        pieces[me, part, :] = value.astype(pieces.dtype)
        sent = []
        for k, peer in enumerate(layer_peers):
            copy = pltpu.make_async_remote_copy(
                src_ref=pieces.at[me, pl.ds(step * rows, rows), :],
                dst_ref=pieces.at[me, pl.ds(step * rows, rows), :],
                send_sem=layer_send.at[k, step],
                recv_sem=layer_recv.at[k, step],
                device_id={"layer": peer},
                device_id_type=MESH,
            )
            copy.start()
            sent.append(copy)
        layer_copies.append(sent)
        if step == 0:
            fit_copy.wait()
        if step > 0:
            for copy in layer_copies[step - 1]:
                copy.wait_recv()
            multiply(step - 1)
    for copy in layer_copies[steps - 1]:
        copy.wait_recv()
    multiply(steps - 1)

    padded = product.shape[2]
    cuts = [0, padded // 256 * 128, padded]
    if width < padded:
        product[:, :, padded - 128 :] = jnp.zeros((peers, out_rows, 128), product.dtype)
    end_copies = []
    for cut in range(2):
        lanes = slice(cuts[cut], min(cuts[cut + 1], width))
        for peer in range(peers):
            product[peer, :, lanes] = total[
                peer * out_rows : (peer + 1) * out_rows, lanes
            ].astype(product.dtype)
        sent = []
        for k, peer in enumerate(row_peers):
            span = pl.ds(cuts[cut], cuts[cut + 1] - cuts[cut])
            copy = pltpu.make_async_remote_copy(
                src_ref=product.at[peer, :, span],
                dst_ref=landed.at[k, :, span],
                send_sem=end_send.at[k, cut],
                recv_sem=end_recv.at[k, cut],
                device_id={"row": peer},
                device_id_type=MESH,
            )
            copy.start()
            sent.append(copy)
        end_copies.append(sent)
    for cut in range(2):
        lanes = slice(cuts[cut], min(cuts[cut + 1], width))
        for copy in end_copies[cut]:
            copy.wait_recv()
        value = total[pl.ds(pl.multiple_of(row * out_rows, out_rows), out_rows), lanes]
        for k in range(peers - 1):
            value = value + landed[k, :, lanes].astype(jnp.float32)
        out_ref[:, lanes] = value.astype(out_ref.dtype)

    for copy in core_copies:
        copy.wait_send()
    for copies in (row_copies, layer_copies, end_copies):
        for sent in copies:
            for copy in sent:
                copy.wait_send()


def exchange(partial, fitting):
    _, peers, piece_rows, half_columns = partial.shape
    depth, width = fitting.shape
    columns = 2 * half_columns
    out_rows = columns // peers
    padded = -(-width // 128) * 128
    steps = 4
    dma = pltpu.SemaphoreType.DMA
    return pl.pallas_call(
        functools.partial(exchange_kernel, peers),
        out_shape=jax.ShapeDtypeStruct((out_rows, width), jnp.bfloat16),
        in_specs=[pl.BlockSpec(memory_space=pltpu.VMEM), pl.BlockSpec(memory_space=pl.ANY)],
        out_specs=pl.BlockSpec(memory_space=pltpu.VMEM),
        scratch_shapes=[
            pltpu.VMEM((depth, width), jnp.bfloat16),
            pltpu.VMEM((peers, piece_rows, half_columns), jnp.bfloat16),
            pltpu.VMEM((peers, piece_rows, half_columns), jnp.bfloat16),
            pltpu.VMEM((peers - 1, piece_rows, half_columns), jnp.bfloat16),
            pltpu.VMEM((4, piece_rows, half_columns), jnp.bfloat16),
            pltpu.VMEM((columns, width), jnp.float32),
            pltpu.VMEM((peers, out_rows, padded), jnp.bfloat16),
            pltpu.VMEM((peers - 1, out_rows, padded), jnp.bfloat16),
            dma,
            dma((steps,)),
            dma((steps,)),
            dma((peers - 1, steps)),
            dma((peers - 1, steps)),
            dma((3, steps)),
            dma((3, steps)),
            dma((peers - 1, 2)),
            dma((peers - 1, 2)),
        ],
        compiler_params=pltpu.CompilerParams(collective_id=0, has_side_effects=True),
    )(partial, fitting)


def local_reduced(layers, table, fitting, owner, local_slice, block_index, weight_index):
    columns = layers.shape[2]
    slice_rows = table.shape[1]
    peer_count = lax.axis_size("row")
    owned_slices = fitting.shape[0] // slice_rows
    half_slices = owned_slices // 2
    half_columns = columns // 2
    slice_total = peer_count * owned_slices
    me = lax.axis_index("layer")
    along = me // 2
    swap_x = [(0, 2), (2, 0), (1, 3), (3, 1)]

    local_now = local_slice[0]
    place = (
        (local_now // half_slices) * (peer_count * half_slices)
        + owner[0, :, 0] * half_slices
        + local_now % half_slices
    )
    meta = jnp.stack([place, block_index[0], weight_index[0]])
    own = lax.dynamic_slice_in_dim(layers[0], along * half_columns, half_columns, 1)
    other = lax.dynamic_slice_in_dim(layers[0], (1 - along) * half_columns, half_columns, 1)
    got = lax.ppermute(other, "layer", swap_x)
    got_meta = lax.ppermute(meta, "layer", swap_x)
    partial = pl.pallas_call(
        terms_kernel,
        out_shape=jax.ShapeDtypeStruct((slice_total, slice_rows, half_columns), jnp.bfloat16),
        in_specs=[pl.BlockSpec(memory_space=pltpu.VMEM)] * 3
        + [pl.BlockSpec(memory_space=pltpu.SMEM)],
        out_specs=pl.BlockSpec(memory_space=pltpu.VMEM),
        scratch_shapes=[pltpu.VMEM((slice_total, slice_rows, half_columns), jnp.float32)],
    )(own, got, table, jnp.stack([meta, got_meta]))
    partial = partial.reshape(2, peer_count, half_slices * slice_rows, half_columns)
    return exchange(partial, fitting)


def local(layers, table, fitting, owner, local_slice, block_index, weight_index):
    arguments = (layers, table, fitting, owner, local_slice, block_index, weight_index)
    entries, peers, group = owner.shape[1], lax.axis_size("row"), lax.axis_size("layer")
    raw_rows = max(2, 2 * entries // peers) * table.shape[2]
    reduced_rows = fitting.shape[0] // group
    if group == 4 and raw_rows > reduced_rows:
        return local_reduced(*arguments)
    return local_rows(*arguments)


def solution(mesh):
    return jax.shard_map(
        local,
        mesh=mesh,
        in_specs=(
            P("layer", "row", "panel"),
            P(),
            P("row", "layer"),
            P("layer", "row", None),
            P("layer", "row"),
            P("layer", "row"),
            P("layer", "row"),
        ),
        out_specs=P(("panel", "row"), "layer"),
        check_vma=False,
    )
```

```python
import functools

import jax
import jax.numpy as jnp
from jax import lax
from jax.experimental import pallas as pl
from jax.experimental.pallas import tpu as pltpu

MESH = pl.DeviceIdType.MESH
from jax.sharding import PartitionSpec as P


def local_rows(layers, table, fitting, owner, local_slice, block_index, weight_index):
    rows_dev = layers.shape[1]
    columns = layers.shape[2]
    slice_rows = table.shape[1]
    block_rows = table.shape[2]
    entries = owner.shape[1]
    peer_count = lax.axis_size("row")
    capacity = max(2, 2 * entries // peer_count)
    slot_count = peer_count * capacity
    owned_slices = fitting.shape[0] // slice_rows
    owner_now = owner[0, :, 0]
    local_now = local_slice[0]
    owner_match = (owner_now[:, None] == jnp.arange(peer_count, dtype=jnp.int32)[None, :]).astype(
        jnp.int32
    )
    slot_rank = jnp.sum((jnp.cumsum(owner_match, axis=0) - 1) * owner_match, axis=1)
    target = owner_now * capacity + slot_rank
    placed = target[None, :] == jnp.arange(slot_count, dtype=jnp.int32)[:, None]
    filled = jnp.any(placed, axis=1)
    source = jnp.sum(jnp.where(placed, jnp.arange(entries, dtype=jnp.int32)[None, :], 0), axis=1)
    send_local = jnp.where(filled, local_now[source], -1).reshape(peer_count, capacity)
    grouped = layers[0].reshape(rows_dev // block_rows, block_rows, columns)
    picked = grouped[block_index[0][source]].reshape(peer_count, capacity, block_rows, columns)
    send_weight = weight_index[0][source].reshape(peer_count, capacity)
    got_rows, got_weight, got_local = (
        lax.all_to_all(picked, "row", split_axis=0, concat_axis=0, tiled=True),
        lax.all_to_all(send_weight, "row", split_axis=0, concat_axis=0, tiled=True),
        lax.all_to_all(send_local, "row", split_axis=0, concat_axis=0, tiled=True),
    )
    pupil_terms = jnp.einsum(
        "ksb,kbc->ksc",
        table[got_weight.reshape(-1)],
        got_rows.reshape(slot_count, block_rows, columns),
        preferred_element_type=jnp.float32,
    ).astype(jnp.bfloat16)
    selector = (
        jnp.arange(owned_slices, dtype=jnp.int32)[:, None] == got_local.reshape(-1)[None, :]
    ).astype(jnp.bfloat16)
    partial_pupil = jnp.dot(
        selector,
        pupil_terms.reshape(slot_count, slice_rows * columns),
        preferred_element_type=jnp.float32,
    ).reshape(owned_slices * slice_rows, columns)
    pupil_rounded = lax.psum(partial_pupil, "layer").astype(jnp.bfloat16)
    return lax.psum_scatter(
        lax.dot_general(
            pupil_rounded, fitting, (((0,), (0,)), ((), ())), preferred_element_type=jnp.float32
        ),
        "row",
        scatter_dimension=0,
        tiled=True,
    ).astype(jnp.bfloat16)


def terms_kernel(own_ref, got_ref, table_ref, meta_ref, out_ref, total_ref):
    entries = meta_ref.shape[2]
    block_rows = table_ref.shape[2]
    total_ref[...] = jnp.zeros_like(total_ref)
    group = 8 if entries % 8 == 0 else 1
    for part, rows_ref in enumerate((own_ref, got_ref)):

        def step(index, carry):
            terms = []
            for offset in range(group):
                entry = index * group + offset
                start = pl.multiple_of(meta_ref[part, 1, entry] * block_rows, block_rows)
                terms.append(
                    jnp.dot(
                        table_ref[meta_ref[part, 2, entry]],
                        rows_ref[pl.ds(start, block_rows), :],
                        preferred_element_type=jnp.float32,
                    )
                )
            for offset in range(group):
                place = meta_ref[part, 0, index * group + offset]
                total_ref[place] += terms[offset]
            return carry

        lax.fori_loop(0, entries // group, step, 0)

    def write(index, carry):
        out_ref[index] = total_ref[index].astype(out_ref.dtype)
        return carry

    lax.fori_loop(0, out_ref.shape[0], write, 0)


def exchange_kernel(
    peers, part_ref, fitting_ref, out_ref,
    fit, core_in, both, row_in, pieces, total, product, landed,
    fit_sem, core_send, core_recv, row_send, row_recv, layer_send, layer_recv, end_send, end_recv,
):
    row = lax.axis_index("row")
    me = lax.axis_index("layer")
    core = lax.rem(me, 2)
    steps = core_send.shape[0]
    piece_rows = pieces.shape[1]
    rows = piece_rows // steps
    width = fit.shape[1]
    half_columns = pieces.shape[2]
    out_rows = out_ref.shape[0]
    mate = row + 1 - 2 * lax.rem(row, 2)
    cross = lax.rem(row + 2, peers)
    opposite = peers - 1 - row
    is_end = jnp.logical_or(row == 0, row == peers - 1)
    is_middle = jnp.logical_not(is_end)
    layer_peers = [lax.rem(me + k, 4) for k in range(1, 4)]

    fit_copy = pltpu.make_async_copy(fitting_ref, fit, fit_sem)
    fit_copy.start()
    barrier = pltpu.get_barrier_semaphore()
    for peer in (mate, cross, opposite):
        pl.semaphore_signal(barrier, inc=1, device_id={"row": peer}, device_id_type=MESH)
    for peer in layer_peers:
        pl.semaphore_signal(barrier, inc=1, device_id={"layer": peer}, device_id_type=MESH)
    pl.semaphore_wait(barrier, peers - 1 + 3)

    core_copies = []
    for step in range(steps):
        copy = pltpu.make_async_remote_copy(
            src_ref=part_ref.at[1 - core, :, pl.ds(step * rows, rows), :],
            dst_ref=core_in.at[:, pl.ds(step * rows, rows), :],
            send_sem=core_send.at[step],
            recv_sem=core_recv.at[step],
            device_id={"layer": me + 1 - 2 * core},
            device_id_type=MESH,
        )
        copy.start()
        core_copies.append(copy)

    def row_copy(slot, step, source, peer):
        part = pl.ds(step * rows, rows)
        return pltpu.make_async_remote_copy(
            src_ref=both.at[source, part, :],
            dst_ref=row_in.at[slot, part, :],
            send_sem=row_send.at[slot, step],
            recv_sem=row_recv.at[slot, step],
            device_id={"row": peer},
            device_id_type=MESH,
        )

    for step in range(steps):
        part = slice(step * rows, (step + 1) * rows)
        core_copies[step].wait_recv()
        both[:, part, :] = (
            part_ref[core, :, part, :].astype(jnp.float32) + core_in[:, part, :].astype(jnp.float32)
        ).astype(both.dtype)

        @pl.when(is_end)
        def _():
            row_copy(3, step, opposite, mate).start()
            row_copy(1, step, cross, cross).start()

        @pl.when(is_middle)
        def _():
            row_copy(2, step, opposite, opposite).start()

        row_copy(0, step, mate, mate).start()

    def join(step):
        part = slice(step * rows, (step + 1) * rows)

        @pl.when(is_middle)
        def _():
            row_copy(3, step, opposite, mate).wait_recv()
            both[cross, part, :] = (
                both[cross, part, :].astype(jnp.float32) + row_in[3, part, :].astype(jnp.float32)
            ).astype(both.dtype)
            row_copy(1, step, cross, cross).start()

    tiles = [(start, min(start + 512, width)) for start in range(0, width, 512)]

    def multiply(step):
        for start, stop in tiles:
            value = None
            for half in range(2):
                part = slice(step * rows, (step + 1) * rows)
                left = jnp.concatenate([pieces[half, part, :], pieces[2 + half, part, :]], axis=1)
                first = half * piece_rows + step * rows
                term = lax.dot_general(
                    left,
                    fit[first : first + rows, start:stop],
                    (((0,), (0,)), ((), ())),
                    preferred_element_type=jnp.float32,
                )
                value = term if value is None else value + term
            if step == 0:
                total[:, start:stop] = value
            else:
                total[:, start:stop] += value

    layer_copies = []
    join(0)
    for step in range(steps):
        part = slice(step * rows, (step + 1) * rows)
        row_copy(0, step, mate, mate).wait_recv()
        row_copy(1, step, cross, cross).wait_recv()

        @pl.when(is_end)
        def _():
            value = both[row, part, :].astype(jnp.float32)
            for slot in range(2):
                value = value + row_in[slot, part, :].astype(jnp.float32)
            pieces[me, part, :] = value.astype(pieces.dtype)

        @pl.when(is_middle)
        def _():
            row_copy(2, step, opposite, opposite).wait_recv()
            value = both[row, part, :].astype(jnp.float32)
            for slot in range(3):
                value = value + row_in[slot, part, :].astype(jnp.float32)
            pieces[me, part, :] = value.astype(pieces.dtype)

        sent = []
        for k, peer in enumerate(layer_peers):
            copy = pltpu.make_async_remote_copy(
                src_ref=pieces.at[me, pl.ds(step * rows, rows), :],
                dst_ref=pieces.at[me, pl.ds(step * rows, rows), :],
                send_sem=layer_send.at[k, step],
                recv_sem=layer_recv.at[k, step],
                device_id={"layer": peer},
                device_id_type=MESH,
            )
            copy.start()
            sent.append(copy)
        layer_copies.append(sent)
        if step + 1 < steps:
            join(step + 1)
        if step == 0:
            fit_copy.wait()
        if step > 0:
            for copy in layer_copies[step - 1]:
                copy.wait_recv()
            multiply(step - 1)
    for copy in layer_copies[steps - 1]:
        copy.wait_recv()
    multiply(steps - 1)

    padded = product.shape[2]
    pieces_out = end_send.shape[1]
    cuts = [padded // 128 * cut // pieces_out * 128 for cut in range(pieces_out + 1)]
    if width < padded:
        product[:, :, padded - 128 :] = jnp.zeros((peers, out_rows, 128), product.dtype)

    def end_copy(slot, cut, source, peer):
        span = pl.ds(cuts[cut], cuts[cut + 1] - cuts[cut])
        return pltpu.make_async_remote_copy(
            src_ref=product.at[source, :, span],
            dst_ref=landed.at[slot, :, span],
            send_sem=end_send.at[slot, cut],
            recv_sem=end_recv.at[slot, cut],
            device_id={"row": peer},
            device_id_type=MESH,
        )

    def lanes_of(cut):
        return slice(cuts[cut], min(cuts[cut + 1], width))

    def total_of(owner, lanes):
        return total[pl.ds(pl.multiple_of(owner * out_rows, out_rows), out_rows), lanes]

    for cut in range(pieces_out):
        lanes = lanes_of(cut)

        @pl.when(is_end)
        def _():
            for peer in (opposite, cross, mate):
                product[peer, :, lanes] = total_of(peer, lanes).astype(product.dtype)
            end_copy(3, cut, opposite, mate).start()
            end_copy(1, cut, cross, cross).start()
            end_copy(0, cut, mate, mate).start()

        @pl.when(is_middle)
        def _():
            for peer in (opposite, mate):
                product[peer, :, lanes] = total_of(peer, lanes).astype(product.dtype)
            end_copy(2, cut, opposite, opposite).start()
            end_copy(0, cut, mate, mate).start()

    @pl.when(is_middle)
    def _():
        for cut in range(pieces_out):
            lanes = lanes_of(cut)
            end_copy(3, cut, opposite, mate).wait_recv()
            product[cross, :, lanes] = (
                total_of(cross, lanes) + landed[3, :, lanes].astype(jnp.float32)
            ).astype(product.dtype)
            end_copy(1, cut, cross, cross).start()

    for cut in range(pieces_out):
        lanes = lanes_of(cut)
        end_copy(0, cut, mate, mate).wait_recv()
        end_copy(1, cut, cross, cross).wait_recv()

        @pl.when(is_end)
        def _():
            value = total_of(row, lanes)
            for slot in range(2):
                value = value + landed[slot, :, lanes].astype(jnp.float32)
            out_ref[:, lanes] = value.astype(out_ref.dtype)

        @pl.when(is_middle)
        def _():
            end_copy(2, cut, opposite, opposite).wait_recv()
            value = total_of(row, lanes)
            for slot in range(3):
                value = value + landed[slot, :, lanes].astype(jnp.float32)
            out_ref[:, lanes] = value.astype(out_ref.dtype)

    for copy in core_copies:
        copy.wait_send()
    for sent in layer_copies:
        for copy in sent:
            copy.wait_send()

    def finish(copy_of, count):
        for index in range(count):
            copy_of(0, index, mate, mate).wait_send()
            copy_of(1, index, cross, cross).wait_send()

            @pl.when(is_end)
            def _():
                copy_of(3, index, opposite, mate).wait_send()

            @pl.when(is_middle)
            def _():
                copy_of(2, index, opposite, opposite).wait_send()

    finish(row_copy, steps)
    finish(end_copy, pieces_out)


def exchange(partial, fitting):
    _, peers, piece_rows, half_columns = partial.shape
    depth, width = fitting.shape
    columns = 2 * half_columns
    out_rows = columns // peers
    padded = -(-width // 128) * 128
    steps = 4
    dma = pltpu.SemaphoreType.DMA
    return pl.pallas_call(
        functools.partial(exchange_kernel, peers),
        out_shape=jax.ShapeDtypeStruct((out_rows, width), jnp.bfloat16),
        in_specs=[pl.BlockSpec(memory_space=pltpu.VMEM), pl.BlockSpec(memory_space=pl.ANY)],
        out_specs=pl.BlockSpec(memory_space=pltpu.VMEM),
        scratch_shapes=[
            pltpu.VMEM((depth, width), jnp.bfloat16),
            pltpu.VMEM((peers, piece_rows, half_columns), jnp.bfloat16),
            pltpu.VMEM((peers, piece_rows, half_columns), jnp.bfloat16),
            pltpu.VMEM((4, piece_rows, half_columns), jnp.bfloat16),
            pltpu.VMEM((4, piece_rows, half_columns), jnp.bfloat16),
            pltpu.VMEM((columns, width), jnp.float32),
            pltpu.VMEM((peers, out_rows, padded), jnp.bfloat16),
            pltpu.VMEM((4, out_rows, padded), jnp.bfloat16),
            dma,
            dma((steps,)),
            dma((steps,)),
            dma((4, steps)),
            dma((4, steps)),
            dma((3, steps)),
            dma((3, steps)),
            dma((4, 3)),
            dma((4, 3)),
        ],
        compiler_params=pltpu.CompilerParams(collective_id=0, has_side_effects=True),
    )(partial, fitting)


def local_reduced(layers, table, fitting, owner, local_slice, block_index, weight_index):
    columns = layers.shape[2]
    slice_rows = table.shape[1]
    peer_count = lax.axis_size("row")
    owned_slices = fitting.shape[0] // slice_rows
    half_slices = owned_slices // 2
    half_columns = columns // 2
    slice_total = peer_count * owned_slices
    me = lax.axis_index("layer")
    along = me // 2
    swap_x = [(0, 2), (2, 0), (1, 3), (3, 1)]

    local_now = local_slice[0]
    place = (
        (local_now // half_slices) * (peer_count * half_slices)
        + owner[0, :, 0] * half_slices
        + local_now % half_slices
    )
    meta = jnp.stack([place, block_index[0], weight_index[0]])
    own = lax.dynamic_slice_in_dim(layers[0], along * half_columns, half_columns, 1)
    other = lax.dynamic_slice_in_dim(layers[0], (1 - along) * half_columns, half_columns, 1)
    got = lax.ppermute(other, "layer", swap_x)
    got_meta = lax.ppermute(meta, "layer", swap_x)
    partial = pl.pallas_call(
        terms_kernel,
        out_shape=jax.ShapeDtypeStruct((slice_total, slice_rows, half_columns), jnp.bfloat16),
        in_specs=[pl.BlockSpec(memory_space=pltpu.VMEM)] * 3
        + [pl.BlockSpec(memory_space=pltpu.SMEM)],
        out_specs=pl.BlockSpec(memory_space=pltpu.VMEM),
        scratch_shapes=[pltpu.VMEM((slice_total, slice_rows, half_columns), jnp.float32)],
    )(own, got, table, jnp.stack([meta, got_meta]))
    partial = partial.reshape(2, peer_count, half_slices * slice_rows, half_columns)
    return exchange(partial, fitting)


def local(layers, table, fitting, owner, local_slice, block_index, weight_index):
    arguments = (layers, table, fitting, owner, local_slice, block_index, weight_index)
    entries, peers, group = owner.shape[1], lax.axis_size("row"), lax.axis_size("layer")
    raw_rows = max(2, 2 * entries // peers) * table.shape[2]
    reduced_rows = fitting.shape[0] // group
    if group == 4 and peers == 4 and raw_rows > reduced_rows:
        return local_reduced(*arguments)
    return local_rows(*arguments)


def solution(mesh):
    return jax.shard_map(
        local,
        mesh=mesh,
        in_specs=(
            P("layer", "row", "panel"),
            P(),
            P("row", "layer"),
            P("layer", "row", None),
            P("layer", "row"),
            P("layer", "row"),
            P("layer", "row"),
        ),
        out_specs=P(("panel", "row"), "layer"),
        check_vma=False,
    )
```

```python
import functools

import jax
import jax.numpy as jnp
from jax import lax
from jax.experimental import pallas as pl
from jax.experimental.pallas import tpu as pltpu

MESH = pl.DeviceIdType.MESH
from jax.sharding import PartitionSpec as P


def local_rows(layers, table, fitting, owner, local_slice, block_index, weight_index):
    rows_dev = layers.shape[1]
    columns = layers.shape[2]
    slice_rows = table.shape[1]
    block_rows = table.shape[2]
    entries = owner.shape[1]
    peer_count = lax.axis_size("row")
    capacity = max(2, 2 * entries // peer_count)
    slot_count = peer_count * capacity
    owned_slices = fitting.shape[0] // slice_rows
    owner_now = owner[0, :, 0]
    local_now = local_slice[0]
    owner_match = (owner_now[:, None] == jnp.arange(peer_count, dtype=jnp.int32)[None, :]).astype(
        jnp.int32
    )
    slot_rank = jnp.sum((jnp.cumsum(owner_match, axis=0) - 1) * owner_match, axis=1)
    target = owner_now * capacity + slot_rank
    placed = target[None, :] == jnp.arange(slot_count, dtype=jnp.int32)[:, None]
    filled = jnp.any(placed, axis=1)
    source = jnp.sum(jnp.where(placed, jnp.arange(entries, dtype=jnp.int32)[None, :], 0), axis=1)
    send_local = jnp.where(filled, local_now[source], -1).reshape(peer_count, capacity)
    grouped = layers[0].reshape(rows_dev // block_rows, block_rows, columns)
    picked = grouped[block_index[0][source]].reshape(peer_count, capacity, block_rows, columns)
    send_weight = weight_index[0][source].reshape(peer_count, capacity)
    got_rows, got_weight, got_local = (
        lax.all_to_all(picked, "row", split_axis=0, concat_axis=0, tiled=True),
        lax.all_to_all(send_weight, "row", split_axis=0, concat_axis=0, tiled=True),
        lax.all_to_all(send_local, "row", split_axis=0, concat_axis=0, tiled=True),
    )
    pupil_terms = jnp.einsum(
        "ksb,kbc->ksc",
        table[got_weight.reshape(-1)],
        got_rows.reshape(slot_count, block_rows, columns),
        preferred_element_type=jnp.float32,
    ).astype(jnp.bfloat16)
    selector = (
        jnp.arange(owned_slices, dtype=jnp.int32)[:, None] == got_local.reshape(-1)[None, :]
    ).astype(jnp.bfloat16)
    partial_pupil = jnp.dot(
        selector,
        pupil_terms.reshape(slot_count, slice_rows * columns),
        preferred_element_type=jnp.float32,
    ).reshape(owned_slices * slice_rows, columns)
    pupil_rounded = lax.psum(partial_pupil, "layer").astype(jnp.bfloat16)
    return lax.psum_scatter(
        lax.dot_general(
            pupil_rounded, fitting, (((0,), (0,)), ((), ())), preferred_element_type=jnp.float32
        ),
        "row",
        scatter_dimension=0,
        tiled=True,
    ).astype(jnp.bfloat16)


def swap_kernel(
    rows_ref, meta_ref, turned_ref, got_ref, got_meta_ref, table_ref, send_sem, recv_sem
):
    me = lax.axis_index("layer")
    half = got_ref.shape[1]
    partner = lax.rem(me + 2, 4)
    barrier = pltpu.get_barrier_semaphore()
    pl.semaphore_signal(barrier, inc=1, device_id={"layer": partner}, device_id_type=MESH)
    pl.semaphore_wait(barrier, 1)
    first = pl.multiple_of((1 - me // 2) * half, half)
    copies = [
        pltpu.make_async_remote_copy(
            src_ref=source,
            dst_ref=target,
            send_sem=send_sem.at[index],
            recv_sem=recv_sem.at[index],
            device_id={"layer": partner},
            device_id_type=MESH,
        )
        for index, (source, target) in enumerate(
            ((meta_ref, got_meta_ref), (rows_ref.at[:, pl.ds(first, half)], got_ref))
        )
    ]
    for copy in copies:
        copy.start()
    for index in range(table_ref.shape[0]):
        table_ref[index] = turned_ref[index].T
    for copy in copies:
        copy.wait()


def swap(rows, meta, table):
    any_space = pl.BlockSpec(memory_space=pl.ANY)
    vmem = pl.BlockSpec(memory_space=pltpu.VMEM)
    return pl.pallas_call(
        swap_kernel,
        out_shape=(
            jax.ShapeDtypeStruct((rows.shape[0], rows.shape[1] // 2), rows.dtype),
            jax.ShapeDtypeStruct(meta.shape, meta.dtype),
            jax.ShapeDtypeStruct(table.shape, table.dtype),
        ),
        in_specs=[any_space, any_space, vmem],
        out_specs=(any_space, any_space, vmem),
        scratch_shapes=[pltpu.SemaphoreType.DMA((2,)), pltpu.SemaphoreType.DMA((2,))],
        compiler_params=pltpu.CompilerParams(collective_id=1, has_side_effects=True),
    )(rows, meta, table.transpose(0, 2, 1))


def terms_kernel(
    peers, half_slices, own_ref, got_ref, table_ref, meta_ref, got_meta_ref, out_ref, total_ref
):
    entries = meta_ref.shape[1]
    block_rows = table_ref.shape[2]
    half = got_ref.shape[1]
    first = pl.multiple_of(lax.axis_index("layer") // 2 * half, half)
    total_ref[...] = jnp.zeros_like(total_ref)
    group = 8 if entries % 8 == 0 else 1
    for index_ref, rows_ref, lanes in (
        (meta_ref, own_ref, pl.ds(first, half)),
        (got_meta_ref, got_ref, slice(None)),
    ):

        def step(index, carry):
            terms = []
            for offset in range(group):
                entry = index * group + offset
                start = pl.multiple_of(index_ref[2, entry] * block_rows, block_rows)
                terms.append(
                    jnp.dot(
                        table_ref[index_ref[3, entry]],
                        rows_ref[pl.ds(start, block_rows), lanes],
                        preferred_element_type=jnp.float32,
                    )
                )
            for offset in range(group):
                entry = index * group + offset
                local_now = index_ref[1, entry]
                upper = (local_now >= half_slices).astype(jnp.int32)
                place = (upper * (peers - 1) + index_ref[0, entry]) * half_slices + local_now
                total_ref[place] += terms[offset]
            return carry

        lax.fori_loop(0, entries // group, step, 0)

    def write(index, carry):
        out_ref[index] = total_ref[index].astype(out_ref.dtype)
        return carry

    lax.fori_loop(0, out_ref.shape[0], write, 0)


def exchange_kernel(
    peers, part_ref, fitting_ref, out_ref,
    fit, core_in, both, row_in, pieces, total, product, landed,
    fit_sem, core_send, core_recv, row_send, row_recv, layer_send, layer_recv, end_send, end_recv,
):
    row = lax.axis_index("row")
    me = lax.axis_index("layer")
    core = lax.rem(me, 2)
    steps = core_send.shape[0]
    piece_rows = pieces.shape[1]
    rows = piece_rows // steps
    width = fit.shape[0]
    half_columns = pieces.shape[2]
    out_rows = out_ref.shape[0]
    mate = row + 1 - 2 * lax.rem(row, 2)
    cross = lax.rem(row + 2, peers)
    opposite = peers - 1 - row
    is_end = jnp.logical_or(row == 0, row == peers - 1)
    is_middle = jnp.logical_not(is_end)
    layer_peers = [lax.rem(me + k, 4) for k in range(1, 4)]

    fit_copy = pltpu.make_async_copy(fitting_ref, fit, fit_sem)
    fit_copy.start()
    barrier = pltpu.get_barrier_semaphore()
    for peer in (mate, cross, opposite):
        pl.semaphore_signal(barrier, inc=1, device_id={"row": peer}, device_id_type=MESH)
    for peer in layer_peers:
        pl.semaphore_signal(barrier, inc=1, device_id={"layer": peer}, device_id_type=MESH)
    pl.semaphore_wait(barrier, peers - 1 + 3)

    core_copies = []
    for step in range(steps):
        copy = pltpu.make_async_remote_copy(
            src_ref=part_ref.at[1 - core, :, pl.ds(step * rows, rows), :],
            dst_ref=core_in.at[:, pl.ds(step * rows, rows), :],
            send_sem=core_send.at[step],
            recv_sem=core_recv.at[step],
            device_id={"layer": me + 1 - 2 * core},
            device_id_type=MESH,
        )
        copy.start()
        core_copies.append(copy)

    def row_copy(slot, step, source, peer):
        part = pl.ds(step * rows, rows)
        return pltpu.make_async_remote_copy(
            src_ref=both.at[source, part, :],
            dst_ref=row_in.at[slot, part, :],
            send_sem=row_send.at[slot, step],
            recv_sem=row_recv.at[slot, step],
            device_id={"row": peer},
            device_id_type=MESH,
        )

    for step in range(steps):
        part = slice(step * rows, (step + 1) * rows)
        core_copies[step].wait_recv()
        both[:, part, :] = (
            part_ref[core, :, part, :].astype(jnp.float32) + core_in[:, part, :].astype(jnp.float32)
        ).astype(both.dtype)

        @pl.when(is_end)
        def _():
            row_copy(3, step, opposite, mate).start()
            row_copy(1, step, cross, cross).start()

        @pl.when(is_middle)
        def _():
            row_copy(2, step, opposite, opposite).start()

        row_copy(0, step, mate, mate).start()

    def join(step):
        part = slice(step * rows, (step + 1) * rows)

        @pl.when(is_middle)
        def _():
            row_copy(3, step, opposite, mate).wait_recv()
            both[cross, part, :] = (
                both[cross, part, :].astype(jnp.float32) + row_in[3, part, :].astype(jnp.float32)
            ).astype(both.dtype)
            row_copy(1, step, cross, cross).start()

    tiles = [(start, min(start + 512, width)) for start in range(0, width, 512)]

    def multiply(step):
        for start, stop in tiles:
            value = None
            for half in range(2):
                part = slice(step * rows, (step + 1) * rows)
                left = jnp.concatenate([pieces[half, part, :], pieces[2 + half, part, :]], axis=1)
                first = half * piece_rows + step * rows
                term = lax.dot_general(
                    left,
                    fit[start:stop, first : first + rows],
                    (((0,), (1,)), ((), ())),
                    preferred_element_type=jnp.float32,
                )
                value = term if value is None else value + term
            if step == 0:
                total[:, start:stop] = value
            else:
                total[:, start:stop] += value

    layer_copies = []
    join(0)
    for step in range(steps):
        part = slice(step * rows, (step + 1) * rows)
        row_copy(0, step, mate, mate).wait_recv()
        row_copy(1, step, cross, cross).wait_recv()

        @pl.when(is_end)
        def _():
            value = both[row, part, :].astype(jnp.float32)
            for slot in range(2):
                value = value + row_in[slot, part, :].astype(jnp.float32)
            pieces[me, part, :] = value.astype(pieces.dtype)

        @pl.when(is_middle)
        def _():
            row_copy(2, step, opposite, opposite).wait_recv()
            value = both[row, part, :].astype(jnp.float32)
            for slot in range(3):
                value = value + row_in[slot, part, :].astype(jnp.float32)
            pieces[me, part, :] = value.astype(pieces.dtype)

        sent = []
        for k, peer in enumerate(layer_peers):
            copy = pltpu.make_async_remote_copy(
                src_ref=pieces.at[me, pl.ds(step * rows, rows), :],
                dst_ref=pieces.at[me, pl.ds(step * rows, rows), :],
                send_sem=layer_send.at[k, step],
                recv_sem=layer_recv.at[k, step],
                device_id={"layer": peer},
                device_id_type=MESH,
            )
            copy.start()
            sent.append(copy)
        layer_copies.append(sent)
        if step + 1 < steps:
            join(step + 1)
        if step == 0:
            fit_copy.wait()
        if step > 0:
            for copy in layer_copies[step - 1]:
                copy.wait_recv()
            multiply(step - 1)
    for copy in layer_copies[steps - 1]:
        copy.wait_recv()
    multiply(steps - 1)

    padded = product.shape[2]
    pieces_out = end_send.shape[1]
    cuts = [padded // 128 * cut // pieces_out * 128 for cut in range(pieces_out + 1)]
    if width < padded:
        product[:, :, padded - 128 :] = jnp.zeros((peers, out_rows, 128), product.dtype)

    def end_copy(slot, cut, source, peer):
        span = pl.ds(cuts[cut], cuts[cut + 1] - cuts[cut])
        return pltpu.make_async_remote_copy(
            src_ref=product.at[source, :, span],
            dst_ref=landed.at[slot, :, span],
            send_sem=end_send.at[slot, cut],
            recv_sem=end_recv.at[slot, cut],
            device_id={"row": peer},
            device_id_type=MESH,
        )

    def lanes_of(cut):
        return slice(cuts[cut], min(cuts[cut + 1], width))

    def total_of(owner, lanes):
        return total[pl.ds(pl.multiple_of(owner * out_rows, out_rows), out_rows), lanes]

    for cut in range(pieces_out):
        lanes = lanes_of(cut)

        @pl.when(is_end)
        def _():
            for peer in (opposite, cross, mate):
                product[peer, :, lanes] = total_of(peer, lanes).astype(product.dtype)
            end_copy(3, cut, opposite, mate).start()
            end_copy(1, cut, cross, cross).start()
            end_copy(0, cut, mate, mate).start()

        @pl.when(is_middle)
        def _():
            for peer in (opposite, mate):
                product[peer, :, lanes] = total_of(peer, lanes).astype(product.dtype)
            end_copy(2, cut, opposite, opposite).start()
            end_copy(0, cut, mate, mate).start()

    @pl.when(is_middle)
    def _():
        for cut in range(pieces_out):
            lanes = lanes_of(cut)
            end_copy(3, cut, opposite, mate).wait_recv()
            product[cross, :, lanes] = (
                total_of(cross, lanes) + landed[3, :, lanes].astype(jnp.float32)
            ).astype(product.dtype)
            end_copy(1, cut, cross, cross).start()

    for cut in range(pieces_out):
        lanes = lanes_of(cut)
        end_copy(0, cut, mate, mate).wait_recv()
        end_copy(1, cut, cross, cross).wait_recv()

        @pl.when(is_end)
        def _():
            value = total_of(row, lanes)
            for slot in range(2):
                value = value + landed[slot, :, lanes].astype(jnp.float32)
            out_ref[:, lanes] = value.astype(out_ref.dtype)

        @pl.when(is_middle)
        def _():
            end_copy(2, cut, opposite, opposite).wait_recv()
            value = total_of(row, lanes)
            for slot in range(3):
                value = value + landed[slot, :, lanes].astype(jnp.float32)
            out_ref[:, lanes] = value.astype(out_ref.dtype)

    for copy in core_copies:
        copy.wait_send()
    for sent in layer_copies:
        for copy in sent:
            copy.wait_send()

    def finish(copy_of, count):
        for index in range(count):
            copy_of(0, index, mate, mate).wait_send()
            copy_of(1, index, cross, cross).wait_send()

            @pl.when(is_end)
            def _():
                copy_of(3, index, opposite, mate).wait_send()

            @pl.when(is_middle)
            def _():
                copy_of(2, index, opposite, opposite).wait_send()

    finish(row_copy, steps)
    finish(end_copy, pieces_out)


def exchange(partial, fitting):
    _, peers, piece_rows, half_columns = partial.shape
    depth, width = fitting.shape
    columns = 2 * half_columns
    out_rows = columns // peers
    padded = -(-width // 128) * 128
    steps = 4
    dma = pltpu.SemaphoreType.DMA
    return pl.pallas_call(
        functools.partial(exchange_kernel, peers),
        out_shape=jax.ShapeDtypeStruct((out_rows, width), jnp.bfloat16),
        in_specs=[pl.BlockSpec(memory_space=pltpu.VMEM), pl.BlockSpec(memory_space=pl.ANY)],
        out_specs=pl.BlockSpec(memory_space=pltpu.VMEM),
        scratch_shapes=[
            pltpu.VMEM((width, depth), jnp.bfloat16),
            pltpu.VMEM((peers, piece_rows, half_columns), jnp.bfloat16),
            pltpu.VMEM((peers, piece_rows, half_columns), jnp.bfloat16),
            pltpu.VMEM((4, piece_rows, half_columns), jnp.bfloat16),
            pltpu.VMEM((4, piece_rows, half_columns), jnp.bfloat16),
            pltpu.VMEM((columns, width), jnp.float32),
            pltpu.VMEM((peers, out_rows, padded), jnp.bfloat16),
            pltpu.VMEM((4, out_rows, padded), jnp.bfloat16),
            dma,
            dma((steps,)),
            dma((steps,)),
            dma((4, steps)),
            dma((4, steps)),
            dma((3, steps)),
            dma((3, steps)),
            dma((4, 3)),
            dma((4, 3)),
        ],
        compiler_params=pltpu.CompilerParams(collective_id=0, has_side_effects=True),
    )(partial, fitting.T)


def local_reduced(layers, table, fitting, owner, local_slice, block_index, weight_index):
    columns = layers.shape[2]
    slice_rows = table.shape[1]
    peer_count = lax.axis_size("row")
    owned_slices = fitting.shape[0] // slice_rows
    half_slices = owned_slices // 2
    half_columns = columns // 2
    slice_total = peer_count * owned_slices
    meta = jnp.stack([owner[0, :, 0], local_slice[0], block_index[0], weight_index[0]])
    got, got_meta, turned = swap(layers[0], meta, table)
    partial = pl.pallas_call(
        functools.partial(terms_kernel, peer_count, half_slices),
        out_shape=jax.ShapeDtypeStruct((slice_total, slice_rows, half_columns), jnp.bfloat16),
        in_specs=[pl.BlockSpec(memory_space=pltpu.VMEM)] * 3
        + [pl.BlockSpec(memory_space=pltpu.SMEM)] * 2,
        out_specs=pl.BlockSpec(memory_space=pltpu.VMEM),
        scratch_shapes=[pltpu.VMEM((slice_total, slice_rows, half_columns), jnp.float32)],
    )(layers[0], got, turned, meta, got_meta)
    partial = partial.reshape(2, peer_count, half_slices * slice_rows, half_columns)
    return exchange(partial, fitting)


def local(layers, table, fitting, owner, local_slice, block_index, weight_index):
    arguments = (layers, table, fitting, owner, local_slice, block_index, weight_index)
    entries, peers, group = owner.shape[1], lax.axis_size("row"), lax.axis_size("layer")
    raw_rows = max(2, 2 * entries // peers) * table.shape[2]
    reduced_rows = fitting.shape[0] // group
    if group == 4 and peers == 4 and raw_rows > reduced_rows:
        return local_reduced(*arguments)
    return local_rows(*arguments)


def solution(mesh):
    return jax.shard_map(
        local,
        mesh=mesh,
        in_specs=(
            P("layer", "row", "panel"),
            P(),
            P("row", "layer"),
            P("layer", "row", None),
            P("layer", "row"),
            P("layer", "row"),
            P("layer", "row"),
        ),
        out_specs=P(("panel", "row"), "layer"),
        check_vma=False,
    )
```

```python
import functools

import jax
import jax.numpy as jnp
from jax import lax
from jax.experimental import pallas as pl
from jax.experimental.pallas import tpu as pltpu

MESH = pl.DeviceIdType.MESH
from jax.sharding import PartitionSpec as P


def local_rows(layers, table, fitting, owner, local_slice, block_index, weight_index):
    rows_dev = layers.shape[1]
    columns = layers.shape[2]
    slice_rows = table.shape[1]
    block_rows = table.shape[2]
    entries = owner.shape[1]
    peer_count = lax.axis_size("row")
    capacity = max(2, 2 * entries // peer_count)
    slot_count = peer_count * capacity
    owned_slices = fitting.shape[0] // slice_rows
    owner_now = owner[0, :, 0]
    local_now = local_slice[0]
    owner_match = (owner_now[:, None] == jnp.arange(peer_count, dtype=jnp.int32)[None, :]).astype(
        jnp.int32
    )
    slot_rank = jnp.sum((jnp.cumsum(owner_match, axis=0) - 1) * owner_match, axis=1)
    target = owner_now * capacity + slot_rank
    placed = target[None, :] == jnp.arange(slot_count, dtype=jnp.int32)[:, None]
    filled = jnp.any(placed, axis=1)
    source = jnp.sum(jnp.where(placed, jnp.arange(entries, dtype=jnp.int32)[None, :], 0), axis=1)
    send_local = jnp.where(filled, local_now[source], -1).reshape(peer_count, capacity)
    grouped = layers[0].reshape(rows_dev // block_rows, block_rows, columns)
    picked = grouped[block_index[0][source]].reshape(peer_count, capacity, block_rows, columns)
    send_weight = weight_index[0][source].reshape(peer_count, capacity)
    got_rows, got_weight, got_local = (
        lax.all_to_all(picked, "row", split_axis=0, concat_axis=0, tiled=True),
        lax.all_to_all(send_weight, "row", split_axis=0, concat_axis=0, tiled=True),
        lax.all_to_all(send_local, "row", split_axis=0, concat_axis=0, tiled=True),
    )
    pupil_terms = jnp.einsum(
        "ksb,kbc->ksc",
        table[got_weight.reshape(-1)],
        got_rows.reshape(slot_count, block_rows, columns),
        preferred_element_type=jnp.float32,
    ).astype(jnp.bfloat16)
    selector = (
        jnp.arange(owned_slices, dtype=jnp.int32)[:, None] == got_local.reshape(-1)[None, :]
    ).astype(jnp.bfloat16)
    partial_pupil = jnp.dot(
        selector,
        pupil_terms.reshape(slot_count, slice_rows * columns),
        preferred_element_type=jnp.float32,
    ).reshape(owned_slices * slice_rows, columns)
    pupil_rounded = lax.psum(partial_pupil, "layer").astype(jnp.bfloat16)
    return lax.psum_scatter(
        lax.dot_general(
            pupil_rounded, fitting, (((0,), (0,)), ((), ())), preferred_element_type=jnp.float32
        ),
        "row",
        scatter_dimension=0,
        tiled=True,
    ).astype(jnp.bfloat16)


def swap_kernel(
    rows_ref, meta_ref, turned_ref, got_ref, got_meta_ref, table_ref, send_sem, recv_sem
):
    me = lax.axis_index("layer")
    half = got_ref.shape[1]
    partner = lax.rem(me + 2, 4)
    barrier = pltpu.get_barrier_semaphore()
    pl.semaphore_signal(barrier, inc=1, device_id={"layer": partner}, device_id_type=MESH)
    pl.semaphore_wait(barrier, 1)
    first = pl.multiple_of((1 - me // 2) * half, half)
    copies = [
        pltpu.make_async_remote_copy(
            src_ref=source,
            dst_ref=target,
            send_sem=send_sem.at[index],
            recv_sem=recv_sem.at[index],
            device_id={"layer": partner},
            device_id_type=MESH,
        )
        for index, (source, target) in enumerate(
            ((meta_ref, got_meta_ref), (rows_ref.at[:, pl.ds(first, half)], got_ref))
        )
    ]
    for copy in copies:
        copy.start()
    for index in range(table_ref.shape[0]):
        table_ref[index] = turned_ref[index].T
    for copy in copies:
        copy.wait()


def swap(rows, meta, table):
    any_space = pl.BlockSpec(memory_space=pl.ANY)
    vmem = pl.BlockSpec(memory_space=pltpu.VMEM)
    return pl.pallas_call(
        swap_kernel,
        out_shape=(
            jax.ShapeDtypeStruct((rows.shape[0], rows.shape[1] // 2), rows.dtype),
            jax.ShapeDtypeStruct(meta.shape, meta.dtype),
            jax.ShapeDtypeStruct(table.shape, table.dtype),
        ),
        in_specs=[any_space, any_space, vmem],
        out_specs=(any_space, any_space, vmem),
        scratch_shapes=[pltpu.SemaphoreType.DMA((2,)), pltpu.SemaphoreType.DMA((2,))],
        compiler_params=pltpu.CompilerParams(collective_id=1, has_side_effects=True),
    )(rows, meta, table.transpose(0, 2, 1))


def terms_kernel(
    peers, half_slices, own_ref, got_ref, table_ref, meta_ref, got_meta_ref, out_ref, total_ref
):
    entries = meta_ref.shape[1]
    block_rows = table_ref.shape[2]
    half = got_ref.shape[1]
    first = pl.multiple_of(lax.axis_index("layer") // 2 * half, half)
    total_ref[...] = jnp.zeros_like(total_ref)
    group = 16 if entries % 16 == 0 else 1
    for index_ref, rows_ref, lanes in (
        (meta_ref, own_ref, pl.ds(first, half)),
        (got_meta_ref, got_ref, slice(None)),
    ):

        def step(index, carry):
            terms = []
            for offset in range(group):
                entry = index * group + offset
                start = pl.multiple_of(index_ref[2, entry] * block_rows, block_rows)
                terms.append(
                    jnp.dot(
                        table_ref[index_ref[3, entry]],
                        rows_ref[pl.ds(start, block_rows), lanes],
                        preferred_element_type=jnp.float32,
                    )
                )
            for offset in range(group):
                entry = index * group + offset
                local_now = index_ref[1, entry]
                upper = (local_now >= half_slices).astype(jnp.int32)
                place = (upper * (peers - 1) + index_ref[0, entry]) * half_slices + local_now
                total_ref[place] += terms[offset]
            return carry

        lax.fori_loop(0, entries // group, step, 0)

    def write(index, carry):
        out_ref[index] = total_ref[index].astype(out_ref.dtype)
        return carry

    lax.fori_loop(0, out_ref.shape[0], write, 0, unroll=4)


def exchange_kernel(
    peers, part_ref, fitting_ref, out_ref,
    fit, core_in, both, row_in, pieces, total, product, landed,
    fit_sem, core_send, core_recv, row_send, row_recv, layer_send, layer_recv, end_send, end_recv,
):
    row = lax.axis_index("row")
    me = lax.axis_index("layer")
    core = lax.rem(me, 2)
    steps = core_send.shape[0]
    piece_rows = pieces.shape[1]
    rows = piece_rows // steps
    width = fit.shape[0]
    half_columns = pieces.shape[2]
    out_rows = out_ref.shape[0]
    mate = row + 1 - 2 * lax.rem(row, 2)
    cross = lax.rem(row + 2, peers)
    opposite = peers - 1 - row
    is_end = jnp.logical_or(row == 0, row == peers - 1)
    is_middle = jnp.logical_not(is_end)
    layer_peers = [lax.rem(me + k, 4) for k in range(1, 4)]

    fit_copy = pltpu.make_async_copy(fitting_ref, fit, fit_sem)
    fit_copy.start()
    barrier = pltpu.get_barrier_semaphore()
    for peer in (mate, cross, opposite):
        pl.semaphore_signal(barrier, inc=1, device_id={"row": peer}, device_id_type=MESH)
    for peer in layer_peers:
        pl.semaphore_signal(barrier, inc=1, device_id={"layer": peer}, device_id_type=MESH)
    pl.semaphore_wait(barrier, peers - 1 + 3)

    core_copies = []
    for step in range(steps):
        copy = pltpu.make_async_remote_copy(
            src_ref=part_ref.at[1 - core, :, pl.ds(step * rows, rows), :],
            dst_ref=core_in.at[:, pl.ds(step * rows, rows), :],
            send_sem=core_send.at[step],
            recv_sem=core_recv.at[step],
            device_id={"layer": me + 1 - 2 * core},
            device_id_type=MESH,
        )
        copy.start()
        core_copies.append(copy)

    def row_copy(slot, step, source, peer):
        part = pl.ds(step * rows, rows)
        return pltpu.make_async_remote_copy(
            src_ref=both.at[source, part, :],
            dst_ref=row_in.at[slot, part, :],
            send_sem=row_send.at[slot, step],
            recv_sem=row_recv.at[slot, step],
            device_id={"row": peer},
            device_id_type=MESH,
        )

    for step in range(steps):
        part = slice(step * rows, (step + 1) * rows)
        core_copies[step].wait_recv()
        both[:, part, :] = (
            part_ref[core, :, part, :].astype(jnp.float32) + core_in[:, part, :].astype(jnp.float32)
        ).astype(both.dtype)

        @pl.when(is_end)
        def _():
            row_copy(3, step, opposite, mate).start()
            row_copy(1, step, cross, cross).start()

        @pl.when(is_middle)
        def _():
            row_copy(2, step, opposite, opposite).start()

        row_copy(0, step, mate, mate).start()

    def join(step):
        part = slice(step * rows, (step + 1) * rows)

        @pl.when(is_middle)
        def _():
            row_copy(3, step, opposite, mate).wait_recv()
            both[cross, part, :] = (
                both[cross, part, :].astype(jnp.float32) + row_in[3, part, :].astype(jnp.float32)
            ).astype(both.dtype)
            row_copy(1, step, cross, cross).start()

    tiles = [(start, min(start + 512, width)) for start in range(0, width, 512)]

    def multiply(step):
        for start, stop in tiles:
            value = None
            for half in range(2):
                part = slice(step * rows, (step + 1) * rows)
                left = jnp.concatenate([pieces[half, part, :], pieces[2 + half, part, :]], axis=1)
                first = half * piece_rows + step * rows
                term = lax.dot_general(
                    left,
                    fit[start:stop, first : first + rows],
                    (((0,), (1,)), ((), ())),
                    preferred_element_type=jnp.float32,
                )
                value = term if value is None else value + term
            if step == 0:
                total[:, start:stop] = value
            else:
                total[:, start:stop] += value

    layer_copies = []
    join(0)
    for step in range(steps):
        part = slice(step * rows, (step + 1) * rows)
        row_copy(0, step, mate, mate).wait_recv()
        row_copy(1, step, cross, cross).wait_recv()

        @pl.when(is_end)
        def _():
            value = both[row, part, :].astype(jnp.float32)
            for slot in range(2):
                value = value + row_in[slot, part, :].astype(jnp.float32)
            pieces[me, part, :] = value.astype(pieces.dtype)

        @pl.when(is_middle)
        def _():
            row_copy(2, step, opposite, opposite).wait_recv()
            value = both[row, part, :].astype(jnp.float32)
            for slot in range(3):
                value = value + row_in[slot, part, :].astype(jnp.float32)
            pieces[me, part, :] = value.astype(pieces.dtype)

        sent = []
        for k, peer in enumerate(layer_peers):
            copy = pltpu.make_async_remote_copy(
                src_ref=pieces.at[me, pl.ds(step * rows, rows), :],
                dst_ref=pieces.at[me, pl.ds(step * rows, rows), :],
                send_sem=layer_send.at[k, step],
                recv_sem=layer_recv.at[k, step],
                device_id={"layer": peer},
                device_id_type=MESH,
            )
            copy.start()
            sent.append(copy)
        layer_copies.append(sent)
        if step + 1 < steps:
            join(step + 1)
        if step == 0:
            fit_copy.wait()
        if step > 0:
            for copy in layer_copies[step - 1]:
                copy.wait_recv()
            multiply(step - 1)
    for copy in layer_copies[steps - 1]:
        copy.wait_recv()
    multiply(steps - 1)

    padded = product.shape[2]
    pieces_out = end_send.shape[1]
    cuts = [padded // 128 * cut // pieces_out * 128 for cut in range(pieces_out + 1)]
    if width < padded:
        product[:, :, padded - 128 :] = jnp.zeros((peers, out_rows, 128), product.dtype)

    def end_copy(slot, cut, source, peer):
        span = pl.ds(cuts[cut], cuts[cut + 1] - cuts[cut])
        return pltpu.make_async_remote_copy(
            src_ref=product.at[source, :, span],
            dst_ref=landed.at[slot, :, span],
            send_sem=end_send.at[slot, cut],
            recv_sem=end_recv.at[slot, cut],
            device_id={"row": peer},
            device_id_type=MESH,
        )

    def lanes_of(cut):
        return slice(cuts[cut], min(cuts[cut + 1], width))

    def total_of(owner, lanes):
        return total[pl.ds(pl.multiple_of(owner * out_rows, out_rows), out_rows), lanes]

    for cut in range(pieces_out):
        lanes = lanes_of(cut)

        @pl.when(is_end)
        def _():
            for peer in (opposite, cross, mate):
                product[peer, :, lanes] = total_of(peer, lanes).astype(product.dtype)
            end_copy(3, cut, opposite, mate).start()
            end_copy(1, cut, cross, cross).start()
            end_copy(0, cut, mate, mate).start()

        @pl.when(is_middle)
        def _():
            for peer in (opposite, mate):
                product[peer, :, lanes] = total_of(peer, lanes).astype(product.dtype)
            end_copy(2, cut, opposite, opposite).start()
            end_copy(0, cut, mate, mate).start()

    @pl.when(is_middle)
    def _():
        for cut in range(pieces_out):
            lanes = lanes_of(cut)
            end_copy(3, cut, opposite, mate).wait_recv()
            product[cross, :, lanes] = (
                total_of(cross, lanes) + landed[3, :, lanes].astype(jnp.float32)
            ).astype(product.dtype)
            end_copy(1, cut, cross, cross).start()

    for cut in range(pieces_out):
        lanes = lanes_of(cut)
        end_copy(0, cut, mate, mate).wait_recv()
        end_copy(1, cut, cross, cross).wait_recv()

        @pl.when(is_end)
        def _():
            value = total_of(row, lanes)
            for slot in range(2):
                value = value + landed[slot, :, lanes].astype(jnp.float32)
            out_ref[:, lanes] = value.astype(out_ref.dtype)

        @pl.when(is_middle)
        def _():
            end_copy(2, cut, opposite, opposite).wait_recv()
            value = total_of(row, lanes)
            for slot in range(3):
                value = value + landed[slot, :, lanes].astype(jnp.float32)
            out_ref[:, lanes] = value.astype(out_ref.dtype)

    for copy in core_copies:
        copy.wait_send()
    for sent in layer_copies:
        for copy in sent:
            copy.wait_send()

    def finish(copy_of, count):
        for index in range(count):
            copy_of(0, index, mate, mate).wait_send()
            copy_of(1, index, cross, cross).wait_send()

            @pl.when(is_end)
            def _():
                copy_of(3, index, opposite, mate).wait_send()

            @pl.when(is_middle)
            def _():
                copy_of(2, index, opposite, opposite).wait_send()

    finish(row_copy, steps)
    finish(end_copy, pieces_out)


def exchange(partial, fitting):
    _, peers, piece_rows, half_columns = partial.shape
    depth, width = fitting.shape
    columns = 2 * half_columns
    out_rows = columns // peers
    padded = -(-width // 128) * 128
    steps = 4
    dma = pltpu.SemaphoreType.DMA
    return pl.pallas_call(
        functools.partial(exchange_kernel, peers),
        out_shape=jax.ShapeDtypeStruct((out_rows, width), jnp.bfloat16),
        in_specs=[pl.BlockSpec(memory_space=pltpu.VMEM), pl.BlockSpec(memory_space=pl.ANY)],
        out_specs=pl.BlockSpec(memory_space=pltpu.VMEM),
        scratch_shapes=[
            pltpu.VMEM((width, depth), jnp.bfloat16),
            pltpu.VMEM((peers, piece_rows, half_columns), jnp.bfloat16),
            pltpu.VMEM((peers, piece_rows, half_columns), jnp.bfloat16),
            pltpu.VMEM((4, piece_rows, half_columns), jnp.bfloat16),
            pltpu.VMEM((4, piece_rows, half_columns), jnp.bfloat16),
            pltpu.VMEM((columns, width), jnp.float32),
            pltpu.VMEM((peers, out_rows, padded), jnp.bfloat16),
            pltpu.VMEM((4, out_rows, padded), jnp.bfloat16),
            dma,
            dma((steps,)),
            dma((steps,)),
            dma((4, steps)),
            dma((4, steps)),
            dma((3, steps)),
            dma((3, steps)),
            dma((4, 3)),
            dma((4, 3)),
        ],
        compiler_params=pltpu.CompilerParams(collective_id=0, has_side_effects=True),
    )(partial, fitting.T)


def local_reduced(layers, table, fitting, owner, local_slice, block_index, weight_index):
    columns = layers.shape[2]
    slice_rows = table.shape[1]
    peer_count = lax.axis_size("row")
    owned_slices = fitting.shape[0] // slice_rows
    half_slices = owned_slices // 2
    half_columns = columns // 2
    slice_total = peer_count * owned_slices
    meta = jnp.stack([owner[0, :, 0], local_slice[0], block_index[0], weight_index[0]])
    got, got_meta, turned = swap(layers[0], meta, table)
    partial = pl.pallas_call(
        functools.partial(terms_kernel, peer_count, half_slices),
        out_shape=jax.ShapeDtypeStruct((slice_total, slice_rows, half_columns), jnp.bfloat16),
        in_specs=[pl.BlockSpec(memory_space=pltpu.VMEM)] * 3
        + [pl.BlockSpec(memory_space=pltpu.SMEM)] * 2,
        out_specs=pl.BlockSpec(memory_space=pltpu.VMEM),
        scratch_shapes=[pltpu.VMEM((slice_total, slice_rows, half_columns), jnp.float32)],
    )(layers[0], got, turned, meta, got_meta)
    partial = partial.reshape(2, peer_count, half_slices * slice_rows, half_columns)
    return exchange(partial, fitting)


def local(layers, table, fitting, owner, local_slice, block_index, weight_index):
    arguments = (layers, table, fitting, owner, local_slice, block_index, weight_index)
    entries, peers, group = owner.shape[1], lax.axis_size("row"), lax.axis_size("layer")
    raw_rows = max(2, 2 * entries // peers) * table.shape[2]
    reduced_rows = fitting.shape[0] // group
    if group == 4 and peers == 4 and raw_rows > reduced_rows:
        return local_reduced(*arguments)
    return local_rows(*arguments)


def solution(mesh):
    return jax.shard_map(
        local,
        mesh=mesh,
        in_specs=(
            P("layer", "row", "panel"),
            P(),
            P("row", "layer"),
            P("layer", "row", None),
            P("layer", "row"),
            P("layer", "row"),
            P("layer", "row"),
        ),
        out_specs=P(("panel", "row"), "layer"),
        check_vma=False,
    )
```

```python
import functools

import jax
import jax.numpy as jnp
from jax import lax
from jax.experimental import pallas as pl
from jax.experimental.pallas import tpu as pltpu

MESH = pl.DeviceIdType.MESH
from jax.sharding import PartitionSpec as P


def local_rows(layers, table, fitting, owner, local_slice, block_index, weight_index):
    rows_dev = layers.shape[1]
    columns = layers.shape[2]
    slice_rows = table.shape[1]
    block_rows = table.shape[2]
    entries = owner.shape[1]
    peer_count = lax.axis_size("row")
    capacity = max(2, 2 * entries // peer_count)
    slot_count = peer_count * capacity
    owned_slices = fitting.shape[0] // slice_rows
    owner_now = owner[0, :, 0]
    local_now = local_slice[0]
    owner_match = (owner_now[:, None] == jnp.arange(peer_count, dtype=jnp.int32)[None, :]).astype(
        jnp.int32
    )
    slot_rank = jnp.sum((jnp.cumsum(owner_match, axis=0) - 1) * owner_match, axis=1)
    target = owner_now * capacity + slot_rank
    placed = target[None, :] == jnp.arange(slot_count, dtype=jnp.int32)[:, None]
    filled = jnp.any(placed, axis=1)
    source = jnp.sum(jnp.where(placed, jnp.arange(entries, dtype=jnp.int32)[None, :], 0), axis=1)
    send_local = jnp.where(filled, local_now[source], -1).reshape(peer_count, capacity)
    grouped = layers[0].reshape(rows_dev // block_rows, block_rows, columns)
    picked = grouped[block_index[0][source]].reshape(peer_count, capacity, block_rows, columns)
    send_weight = weight_index[0][source].reshape(peer_count, capacity)
    got_rows, got_weight, got_local = (
        lax.all_to_all(picked, "row", split_axis=0, concat_axis=0, tiled=True),
        lax.all_to_all(send_weight, "row", split_axis=0, concat_axis=0, tiled=True),
        lax.all_to_all(send_local, "row", split_axis=0, concat_axis=0, tiled=True),
    )
    pupil_terms = jnp.einsum(
        "ksb,kbc->ksc",
        table[got_weight.reshape(-1)],
        got_rows.reshape(slot_count, block_rows, columns),
        preferred_element_type=jnp.float32,
    ).astype(jnp.bfloat16)
    selector = (
        jnp.arange(owned_slices, dtype=jnp.int32)[:, None] == got_local.reshape(-1)[None, :]
    ).astype(jnp.bfloat16)
    partial_pupil = jnp.dot(
        selector,
        pupil_terms.reshape(slot_count, slice_rows * columns),
        preferred_element_type=jnp.float32,
    ).reshape(owned_slices * slice_rows, columns)
    pupil_rounded = lax.psum(partial_pupil, "layer").astype(jnp.bfloat16)
    return lax.psum_scatter(
        lax.dot_general(
            pupil_rounded, fitting, (((0,), (0,)), ((), ())), preferred_element_type=jnp.float32
        ),
        "row",
        scatter_dimension=0,
        tiled=True,
    ).astype(jnp.bfloat16)


def swap_kernel(
    rows_ref, meta_ref, turned_ref, got_ref, got_meta_ref, table_ref, send_sem, recv_sem
):
    me = lax.axis_index("layer")
    half = got_ref.shape[1]
    partner = lax.rem(me + 2, 4)
    barrier = pltpu.get_barrier_semaphore()
    pl.semaphore_signal(barrier, inc=1, device_id={"layer": partner}, device_id_type=MESH)
    pl.semaphore_wait(barrier, 1)
    first = pl.multiple_of((1 - me // 2) * half, half)
    copies = [
        pltpu.make_async_remote_copy(
            src_ref=source,
            dst_ref=target,
            send_sem=send_sem.at[index],
            recv_sem=recv_sem.at[index],
            device_id={"layer": partner},
            device_id_type=MESH,
        )
        for index, (source, target) in enumerate(
            ((meta_ref, got_meta_ref), (rows_ref.at[:, pl.ds(first, half)], got_ref))
        )
    ]
    for copy in copies:
        copy.start()
    for index in range(table_ref.shape[0]):
        table_ref[index] = turned_ref[index].T
    for copy in copies:
        copy.wait()


def swap(rows, meta, table):
    any_space = pl.BlockSpec(memory_space=pl.ANY)
    vmem = pl.BlockSpec(memory_space=pltpu.VMEM)
    return pl.pallas_call(
        swap_kernel,
        out_shape=(
            jax.ShapeDtypeStruct((rows.shape[0], rows.shape[1] // 2), rows.dtype),
            jax.ShapeDtypeStruct(meta.shape, meta.dtype),
            jax.ShapeDtypeStruct(table.shape, table.dtype),
        ),
        in_specs=[any_space, any_space, vmem],
        out_specs=(any_space, any_space, vmem),
        scratch_shapes=[pltpu.SemaphoreType.DMA((2,)), pltpu.SemaphoreType.DMA((2,))],
        compiler_params=pltpu.CompilerParams(collective_id=1, has_side_effects=True),
    )(rows, meta, table.transpose(0, 2, 1))


def terms_kernel(
    peers, half_slices, own_ref, got_ref, table_ref, meta_ref, got_meta_ref, out_ref, total_ref
):
    entries = meta_ref.shape[1]
    block_rows = table_ref.shape[2]
    half = got_ref.shape[1]
    first = pl.multiple_of(lax.axis_index("layer") // 2 * half, half)
    total_ref[...] = jnp.zeros_like(total_ref)
    group = 16 if entries % 16 == 0 else 1
    for index_ref, rows_ref, lanes in (
        (meta_ref, own_ref, pl.ds(first, half)),
        (got_meta_ref, got_ref, slice(None)),
    ):

        def step(index, carry):
            terms = []
            for offset in range(group):
                entry = index * group + offset
                start = pl.multiple_of(index_ref[2, entry] * block_rows, block_rows)
                terms.append(
                    jnp.dot(
                        table_ref[index_ref[3, entry]],
                        rows_ref[pl.ds(start, block_rows), lanes],
                        preferred_element_type=jnp.float32,
                    )
                )
            for offset in range(group):
                entry = index * group + offset
                local_now = index_ref[1, entry]
                upper = (local_now >= half_slices).astype(jnp.int32)
                place = (upper * (peers - 1) + index_ref[0, entry]) * half_slices + local_now
                total_ref[place] += terms[offset]
            return carry

        lax.fori_loop(0, entries // group, step, 0)

    def write(index, carry):
        out_ref[index] = total_ref[index].astype(out_ref.dtype)
        return carry

    lax.fori_loop(0, out_ref.shape[0], write, 0, unroll=4)


def exchange_kernel(
    peers, part_ref, fitting_ref, out_ref,
    fit, kept, core_in, both, row_in, pieces, total, product, landed,
    fit_sem, kept_sem, core_send, core_recv, row_send, row_recv, layer_send, layer_recv, end_send, end_recv,
):
    row = lax.axis_index("row")
    me = lax.axis_index("layer")
    core = lax.rem(me, 2)
    steps = core_send.shape[0]
    piece_rows = pieces.shape[1]
    rows = piece_rows // steps
    width = fit.shape[0]
    half_columns = pieces.shape[2]
    out_rows = out_ref.shape[0]
    mate = row + 1 - 2 * lax.rem(row, 2)
    cross = lax.rem(row + 2, peers)
    opposite = peers - 1 - row
    is_end = jnp.logical_or(row == 0, row == peers - 1)
    is_middle = jnp.logical_not(is_end)
    layer_peers = [lax.rem(me + k, 4) for k in range(1, 4)]

    kept_copy = pltpu.make_async_copy(part_ref.at[core], kept, kept_sem)
    kept_copy.start()
    fit_copy = pltpu.make_async_copy(fitting_ref, fit, fit_sem)
    fit_copy.start()
    barrier = pltpu.get_barrier_semaphore()
    for peer in (mate, cross, opposite):
        pl.semaphore_signal(barrier, inc=1, device_id={"row": peer}, device_id_type=MESH)
    for peer in layer_peers:
        pl.semaphore_signal(barrier, inc=1, device_id={"layer": peer}, device_id_type=MESH)
    pl.semaphore_wait(barrier, peers - 1 + 3)

    core_copies = []
    for step in range(steps):
        copy = pltpu.make_async_remote_copy(
            src_ref=part_ref.at[1 - core, :, pl.ds(step * rows, rows), :],
            dst_ref=core_in.at[:, pl.ds(step * rows, rows), :],
            send_sem=core_send.at[step],
            recv_sem=core_recv.at[step],
            device_id={"layer": me + 1 - 2 * core},
            device_id_type=MESH,
        )
        copy.start()
        core_copies.append(copy)

    def row_copy(slot, step, source, peer):
        part = pl.ds(step * rows, rows)
        return pltpu.make_async_remote_copy(
            src_ref=both.at[source, part, :],
            dst_ref=row_in.at[slot, part, :],
            send_sem=row_send.at[slot, step],
            recv_sem=row_recv.at[slot, step],
            device_id={"row": peer},
            device_id_type=MESH,
        )

    for step in range(steps):
        part = slice(step * rows, (step + 1) * rows)
        if step == 0:
            kept_copy.wait()
        core_copies[step].wait_recv()
        both[:, part, :] = (
            kept[:, part, :].astype(jnp.float32) + core_in[:, part, :].astype(jnp.float32)
        ).astype(both.dtype)

        @pl.when(is_end)
        def _():
            row_copy(3, step, opposite, mate).start()
            row_copy(1, step, cross, cross).start()

        @pl.when(is_middle)
        def _():
            row_copy(2, step, opposite, opposite).start()

        row_copy(0, step, mate, mate).start()

    def join(step):
        part = slice(step * rows, (step + 1) * rows)

        @pl.when(is_middle)
        def _():
            row_copy(3, step, opposite, mate).wait_recv()
            both[cross, part, :] = (
                both[cross, part, :].astype(jnp.float32) + row_in[3, part, :].astype(jnp.float32)
            ).astype(both.dtype)
            row_copy(1, step, cross, cross).start()

    tiles = [(start, min(start + 512, width)) for start in range(0, width, 512)]

    def multiply(step):
        for start, stop in tiles:
            value = None
            for half in range(2):
                part = slice(step * rows, (step + 1) * rows)
                left = jnp.concatenate([pieces[half, part, :], pieces[2 + half, part, :]], axis=1)
                first = half * piece_rows + step * rows
                term = lax.dot_general(
                    left,
                    fit[start:stop, first : first + rows],
                    (((0,), (1,)), ((), ())),
                    preferred_element_type=jnp.float32,
                )
                value = term if value is None else value + term
            if step == 0:
                total[:, start:stop] = value
            else:
                total[:, start:stop] += value

    layer_copies = []
    join(0)
    for step in range(steps):
        part = slice(step * rows, (step + 1) * rows)
        row_copy(0, step, mate, mate).wait_recv()
        row_copy(1, step, cross, cross).wait_recv()

        @pl.when(is_end)
        def _():
            value = both[row, part, :].astype(jnp.float32)
            for slot in range(2):
                value = value + row_in[slot, part, :].astype(jnp.float32)
            pieces[me, part, :] = value.astype(pieces.dtype)

        @pl.when(is_middle)
        def _():
            row_copy(2, step, opposite, opposite).wait_recv()
            value = both[row, part, :].astype(jnp.float32)
            for slot in range(3):
                value = value + row_in[slot, part, :].astype(jnp.float32)
            pieces[me, part, :] = value.astype(pieces.dtype)

        sent = []
        for k, peer in enumerate(layer_peers):
            copy = pltpu.make_async_remote_copy(
                src_ref=pieces.at[me, pl.ds(step * rows, rows), :],
                dst_ref=pieces.at[me, pl.ds(step * rows, rows), :],
                send_sem=layer_send.at[k, step],
                recv_sem=layer_recv.at[k, step],
                device_id={"layer": peer},
                device_id_type=MESH,
            )
            copy.start()
            sent.append(copy)
        layer_copies.append(sent)
        if step + 1 < steps:
            join(step + 1)
        if step == 0:
            fit_copy.wait()
        if step > 0:
            for copy in layer_copies[step - 1]:
                copy.wait_recv()
            multiply(step - 1)
    for copy in layer_copies[steps - 1]:
        copy.wait_recv()
    multiply(steps - 1)

    padded = product.shape[2]
    pieces_out = end_send.shape[1]
    cuts = [padded // 128 * cut // pieces_out * 128 for cut in range(pieces_out + 1)]
    if width < padded:
        product[:, :, padded - 128 :] = jnp.zeros((peers, out_rows, 128), product.dtype)

    def end_copy(slot, cut, source, peer):
        span = pl.ds(cuts[cut], cuts[cut + 1] - cuts[cut])
        return pltpu.make_async_remote_copy(
            src_ref=product.at[source, :, span],
            dst_ref=landed.at[slot, :, span],
            send_sem=end_send.at[slot, cut],
            recv_sem=end_recv.at[slot, cut],
            device_id={"row": peer},
            device_id_type=MESH,
        )

    def lanes_of(cut):
        return slice(cuts[cut], min(cuts[cut + 1], width))

    def total_of(owner, lanes):
        return total[pl.ds(pl.multiple_of(owner * out_rows, out_rows), out_rows), lanes]

    for cut in range(pieces_out):
        lanes = lanes_of(cut)

        @pl.when(is_end)
        def _():
            for peer in (opposite, cross, mate):
                product[peer, :, lanes] = total_of(peer, lanes).astype(product.dtype)
            end_copy(3, cut, opposite, mate).start()
            end_copy(1, cut, cross, cross).start()
            end_copy(0, cut, mate, mate).start()

        @pl.when(is_middle)
        def _():
            for peer in (opposite, mate):
                product[peer, :, lanes] = total_of(peer, lanes).astype(product.dtype)
            end_copy(2, cut, opposite, opposite).start()
            end_copy(0, cut, mate, mate).start()

    @pl.when(is_middle)
    def _():
        for cut in range(pieces_out):
            lanes = lanes_of(cut)
            end_copy(3, cut, opposite, mate).wait_recv()
            product[cross, :, lanes] = (
                total_of(cross, lanes) + landed[3, :, lanes].astype(jnp.float32)
            ).astype(product.dtype)
            end_copy(1, cut, cross, cross).start()

    for cut in range(pieces_out):
        lanes = lanes_of(cut)
        end_copy(0, cut, mate, mate).wait_recv()
        end_copy(1, cut, cross, cross).wait_recv()

        @pl.when(is_end)
        def _():
            value = total_of(row, lanes)
            for slot in range(2):
                value = value + landed[slot, :, lanes].astype(jnp.float32)
            out_ref[:, lanes] = value.astype(out_ref.dtype)

        @pl.when(is_middle)
        def _():
            end_copy(2, cut, opposite, opposite).wait_recv()
            value = total_of(row, lanes)
            for slot in range(3):
                value = value + landed[slot, :, lanes].astype(jnp.float32)
            out_ref[:, lanes] = value.astype(out_ref.dtype)

    for copy in core_copies:
        copy.wait_send()
    for sent in layer_copies:
        for copy in sent:
            copy.wait_send()

    def finish(copy_of, count):
        for index in range(count):
            copy_of(0, index, mate, mate).wait_send()
            copy_of(1, index, cross, cross).wait_send()

            @pl.when(is_end)
            def _():
                copy_of(3, index, opposite, mate).wait_send()

            @pl.when(is_middle)
            def _():
                copy_of(2, index, opposite, opposite).wait_send()

    finish(row_copy, steps)
    finish(end_copy, pieces_out)


def exchange(partial, fitting):
    _, peers, piece_rows, half_columns = partial.shape
    depth, width = fitting.shape
    columns = 2 * half_columns
    out_rows = columns // peers
    padded = -(-width // 128) * 128
    steps = 4
    dma = pltpu.SemaphoreType.DMA
    return pl.pallas_call(
        functools.partial(exchange_kernel, peers),
        out_shape=jax.ShapeDtypeStruct((out_rows, width), jnp.bfloat16),
        in_specs=[pl.BlockSpec(memory_space=pl.ANY), pl.BlockSpec(memory_space=pl.ANY)],
        out_specs=pl.BlockSpec(memory_space=pltpu.VMEM),
        scratch_shapes=[
            pltpu.VMEM((width, depth), jnp.bfloat16),
            pltpu.VMEM((peers, piece_rows, half_columns), jnp.bfloat16),
            pltpu.VMEM((peers, piece_rows, half_columns), jnp.bfloat16),
            pltpu.VMEM((peers, piece_rows, half_columns), jnp.bfloat16),
            pltpu.VMEM((4, piece_rows, half_columns), jnp.bfloat16),
            pltpu.VMEM((4, piece_rows, half_columns), jnp.bfloat16),
            pltpu.VMEM((columns, width), jnp.float32),
            pltpu.VMEM((peers, out_rows, padded), jnp.bfloat16),
            pltpu.VMEM((4, out_rows, padded), jnp.bfloat16),
            dma,
            dma,
            dma((steps,)),
            dma((steps,)),
            dma((4, steps)),
            dma((4, steps)),
            dma((3, steps)),
            dma((3, steps)),
            dma((4, 3)),
            dma((4, 3)),
        ],
        compiler_params=pltpu.CompilerParams(collective_id=0, has_side_effects=True),
    )(partial, fitting.T)


def local_reduced(layers, table, fitting, owner, local_slice, block_index, weight_index):
    columns = layers.shape[2]
    slice_rows = table.shape[1]
    peer_count = lax.axis_size("row")
    owned_slices = fitting.shape[0] // slice_rows
    half_slices = owned_slices // 2
    half_columns = columns // 2
    slice_total = peer_count * owned_slices
    meta = jnp.stack([owner[0, :, 0], local_slice[0], block_index[0], weight_index[0]])
    got, got_meta, turned = swap(layers[0], meta, table)
    partial = pl.pallas_call(
        functools.partial(terms_kernel, peer_count, half_slices),
        out_shape=jax.ShapeDtypeStruct((slice_total, slice_rows, half_columns), jnp.bfloat16),
        in_specs=[pl.BlockSpec(memory_space=pltpu.VMEM)] * 3
        + [pl.BlockSpec(memory_space=pltpu.SMEM)] * 2,
        out_specs=pl.BlockSpec(memory_space=pltpu.VMEM),
        scratch_shapes=[pltpu.VMEM((slice_total, slice_rows, half_columns), jnp.float32)],
    )(layers[0], got, turned, meta, got_meta)
    partial = partial.reshape(2, peer_count, half_slices * slice_rows, half_columns)
    return exchange(partial, fitting)


def local(layers, table, fitting, owner, local_slice, block_index, weight_index):
    arguments = (layers, table, fitting, owner, local_slice, block_index, weight_index)
    entries, peers, group = owner.shape[1], lax.axis_size("row"), lax.axis_size("layer")
    raw_rows = max(2, 2 * entries // peers) * table.shape[2]
    reduced_rows = fitting.shape[0] // group
    if group == 4 and peers == 4 and raw_rows > reduced_rows:
        return local_reduced(*arguments)
    return local_rows(*arguments)


def solution(mesh):
    return jax.shard_map(
        local,
        mesh=mesh,
        in_specs=(
            P("layer", "row", "panel"),
            P(),
            P("row", "layer"),
            P("layer", "row", None),
            P("layer", "row"),
            P("layer", "row"),
            P("layer", "row"),
        ),
        out_specs=P(("panel", "row"), "layer"),
        check_vma=False,
    )
```
